128 devices in a mesh: wide: 16 (over z_lo, x, core), narrow: 8 (over z_hi, y).
Axes of the slice: x: 4, y: 4, z: 4 (z_hi: 2, z_lo: 2; z = z_hi * 2 + z_lo), core: 2. Of those that a mesh axis runs over, the one named last changes fastest.
Arguments:
- vectors: float32 [32000, 8192], P('wide', 'narrow'), may hold values from -0.44860464 to 0.44860464
- reflectors: float32 [32000, 256], P('wide'), may hold values from -6 to 6
- triangle: float32 [256, 256], replicated, may hold values from -3.125e-05 to 7.8125e-05, as said below
- energies: float32 [32000], P('wide'), may hold values from -1 to 1
Outputs:
- updated: float32 [32000, 8192], P('wide', 'narrow')
- fock_block: float32 [8192, 512], P(('narrow', 'wide'))
The draws below stay inside these ranges and needn't reach their ends.
Inputs may be any that keep to these rules, and one draw needn't show every extreme that they name: `triangle`: upper triangular, with diagonal entries between 1.5 / 32000 and 2.5 / 32000 and entries above the diagonal of magnitude at most 1 / 32000.
All inputs are finite; a program needn't handle non-finite values.
Results may differ from the reference program's by a relative error of at most 0.00007.
Values sent between devices are 32-bit elements; how exact they have to be, the bound alone decides.
A program may use at most 64 MiB of HBM per device.

```python
import math
import jax
import jax.numpy as jnp
from jax import lax

NV = 32000
NK = 8192
NB = 256
FB = 512
OFF = 256
N_NARROW = 8


def draw_triangle(key, part):
    key_one, key_two = jax.random.split(key, 2)
    diagonal_part = jax.random.uniform(key_one, (NB,), jnp.float32, 1.5, 2.5)
    upper_part = jnp.clip(jax.random.normal(key_two, (NB, NB), jnp.float32), -4.0, 4.0) * (0.5 / math.sqrt(NB))
    matrix = jnp.triu(upper_part, 1) + jnp.diag(diagonal_part)
    return matrix * (1.0 / NV)


def levels(key, dims, pieces, smallest, top_value):
    level, own = 1.0, jax.random.fold_in(key, 6)
    for position, blocks in pieces:
        heights = jnp.exp(jax.random.uniform(jax.random.fold_in(own, position), (blocks,), jnp.float32, smallest / len(pieces), top_value / len(pieces)))
        level = level * jnp.repeat(heights, dims[position] // blocks).reshape([-1 if axis == position else 1 for axis in range(len(dims))])
    return level


def centred(key, dims, spread, bound, cuts=(), held_as=jnp.bfloat16):
    entries = spread * jax.random.normal(key, dims, jnp.float32)
    if cuts:
        entries = entries * levels(key, dims, cuts, -0.22, 0.18)
    return jnp.clip(entries, -bound, bound).astype(held_as)


def setup_inputs(seed: int = 0) -> dict:
    keys = jax.random.split(jax.random.key(seed), 5)
    return {
        "vectors": centred(keys[0], (NV, NK), (NV ** -0.25), 0.44860464, ((0, 16), (1, 8)), jnp.float32),
        "reflectors": centred(keys[1], (NV, NB), 1.0, 6.0, ((0, 16),), jnp.float32),
        "triangle": draw_triangle(jax.random.fold_in(keys[4], 71), 0),
        "energies": jnp.clip(jax.random.uniform(keys[3], (NV,), jnp.float32, -1.0, 1.0) * levels(keys[3], (NV,), ((0, 16),), -0.4, 0.0), -1.0, 1.0),
    }


def reference(vectors, reflectors, triangle, energies):
    highest = lax.Precision.HIGHEST
    projected = jnp.dot(reflectors.T, vectors, precision=highest, preferred_element_type=jnp.float32)
    coefficients = jnp.dot(triangle, projected, precision=highest, preferred_element_type=jnp.float32)
    updated = vectors - jnp.dot(reflectors, coefficients, precision=highest, preferred_element_type=jnp.float32)
    columns = NK // N_NARROW
    block_width = FB // N_NARROW
    fock_input = updated.reshape(NV, N_NARROW, columns)[:, :, OFF:OFF + block_width].reshape(NV, FB)
    fock_block = jnp.dot(updated.T, energies[:, None] * fock_input, precision=highest, preferred_element_type=jnp.float32)
    return updated, fock_block
```

```python
import functools

import jax
import jax.numpy as jnp
from jax import lax
from jax.experimental import pallas as pl
from jax.experimental.pallas import tpu as pltpu
from jax.sharding import PartitionSpec as P

MESH = pl.DeviceIdType.MESH
F32, BF16 = jnp.float32, jnp.bfloat16
ROWS, KP, NC, NB = 2000, 2048, 1024, 256
FB, OFF, BW = 512, 256, 64


def dot(a, b):
    return jnp.dot(a, b, preferred_element_type=F32)


def split(x):
    hi = x.astype(BF16)
    return hi, (x - hi.astype(F32)).astype(BF16)


def dot3(a, b):
    return dot(a[0], b[0]) + dot(a[0], b[1]) + dot(a[1], b[0])


def mult(i, m):
    return pl.multiple_of(i * m, m)


def kernel(
    v_hbm, r_hbm, t_ref, e_ref, u_hbm, f_ref,
    v, r, vb, rtr, rt, rtt, uu, vbt, pbt, ep, part, xrecv, rsr, pred, pfull, ub, red, fo, fsend,
    ld_sem, out_sem, ag_s, ag_r, xs, xr, rs_s, rs_r, pa_s, pa_r, pr_s, pr_r, pb_s, pb_r, f_s, f_r,
):
    w, n = lax.axis_index("wide"), lax.axis_index("narrow")
    c, k = lax.rem(w, 2), w // 2
    y, zh = lax.rem(n, 4), n // 4
    partner = (w + 1 - 2 * c, n)
    yp, ym = zh * 4 + lax.rem(y + 1, 4), zh * 4 + lax.rem(y + 3, 4)
    base = zh * 4
    zbase = (1 - zh) * 4

    def same_core(kk):
        return (2 * kk + c, n)

    def narrow_peer(nn):
        return (w, nn)

    def remote(src, dst, s, rsem, to):
        return pltpu.make_async_remote_copy(
            src_ref=src, dst_ref=dst, send_sem=s, recv_sem=rsem, device_id=to, device_id_type=MESH
        )

    kk0 = k // 2

    def order(s):
        return lax.rem(kk0 + 1 + s, 4)

    vb_load = pltpu.make_async_copy(v_hbm.at[:, pl.ds(OFF, 128)], vb.at[pl.ds(0, ROWS)], ld_sem.at[0])
    r_load = pltpu.make_async_copy(r_hbm, r.at[pl.ds(0, ROWS)], ld_sem.at[1])

    def v_load(i):
        cols = pl.ds(mult(i, 256), 256)
        return pltpu.make_async_copy(v_hbm.at[:, cols], v.at[pl.ds(0, ROWS), cols], ld_sem.at[2 + i])

    vb_load.start()
    r_load.start()
    for s in range(4):
        v_load(order(s)).start()

    barrier = pltpu.get_barrier_semaphore()
    pl.semaphore_signal(barrier, inc=1, device_id=partner, device_id_type=MESH)
    for d in range(1, 8):
        pl.semaphore_signal(barrier, inc=1, device_id=same_core(lax.rem(k + d, 8)), device_id_type=MESH)
        pl.semaphore_signal(barrier, inc=1, device_id=narrow_peer(lax.rem(n + d, 8)), device_id_type=MESH)

    vb[ROWS:, :] = jnp.zeros((KP - ROWS, 128), F32)
    r[ROWS:, :] = jnp.zeros((KP - ROWS, NB), F32)
    v[ROWS:, :] = jnp.zeros((KP - ROWS, NC), F32)
    ep[...] = jnp.zeros((1, KP), F32)
    ep[:, :ROWS] = e_ref[...]

    vb_load.wait()
    own = pl.ds(mult(n, BW), BW)
    for i in range(KP // 128):
        vbt[own, i * 128 : (i + 1) * 128] = vb[i * 128 : (i + 1) * 128, :].T[:BW, :]
    pl.semaphore_wait(barrier, 15)

    def ag(src_n, half, to, slot):
        rows = pl.ds(mult(src_n * 2 + half, 32), 32)
        return remote(vbt.at[rows], vbt.at[rows], ag_s.at[slot], ag_r.at[src_n * 2 + half], narrow_peer(to))

    zp = zbase + y
    sends = [
        (n, 0, zp, 0), (n, 0, yp, 2), (n, 1, ym, 3), (n, 1, zp, 1), (n, 1, yp, 4), (n, 0, ym, 5),
    ]
    forwards = [(ym, 0, yp, 6), (yp, 1, ym, 7)]
    zsends = [(zp, 0, yp, 8), (zp, 1, ym, 9), (zp, 1, yp, 10), (zp, 0, ym, 11)]
    zym, zyp = zbase + lax.rem(y + 3, 4), zbase + lax.rem(y + 1, 4)
    zforwards = [(zym, 0, yp, 12), (zyp, 1, ym, 13)]

    def ag_arrived(src_n, half):
        ag(src_n, half, yp, 0).wait_recv()

    for m in sends:
        ag(*m).start()

    r_load.wait()

    @pl.loop(0, KP // 128)
    def _(i):
        rows = pl.ds(mult(i, 128), 128)
        for j in range(2):
            hi, lo = split(r[rows, j * 128 : (j + 1) * 128].T)
            rtr[0, j * 128 : (j + 1) * 128, rows] = hi
            rtr[1, j * 128 : (j + 1) * 128, rows] = lo

    myrows = pl.ds(mult(c, 128), 128)
    hisrows = pl.ds(mult(1 - c, 128), 128)

    def x_copy(st, i):
        cols = pl.ds(mult(i, 256), 256)
        return remote(
            part.at[st, hisrows, cols], xrecv.at[st, :, cols], xs.at[st * 4 + i], xr.at[st * 4 + i], partner
        )

    def rs_copy(st, kk):
        return remote(
            part.at[st, myrows, pl.ds(mult(kk, 128), 128)], rsr.at[st, k], rs_s.at[st * 8 + kk],
            rs_r.at[st * 8 + k], same_core(kk),
        )

    def reduce_start(st, compute):
        def finish(i):
            cols = pl.ds(mult(i, 256), 256)
            x_copy(st, i).wait_recv()
            part[st, myrows, cols] = part[st, myrows, cols] + xrecv[st, :, cols]
            for t in range(2):
                kk = 2 * i + t

                @pl.when(kk != k)
                def _():
                    rs_copy(st, kk).start()

        @pl.loop(0, 4)
        def _(s):
            i = order(s)
            part[st, :, pl.ds(mult(i, 256), 256)] = compute(i)
            x_copy(st, i).start()

            @pl.when(s >= 1)
            def _():
                finish(order(s - 1))

        finish(order(3))

    def reduce_end(st):
        total = part[st, myrows, pl.ds(mult(k, 128), 128)]
        for d in range(1, 8):
            kk = lax.rem(k + d, 8)
            remote(rsr.at[st, kk], rsr.at[st, kk], rs_s.at[st * 8], rs_r.at[st * 8 + kk], partner).wait_recv()
            total = total + rsr[st, kk]
        return total

    def reduce_drain(st):
        for i in range(4):
            x_copy(st, i).wait_send()
        for d in range(1, 8):
            rs_copy(st, lax.rem(k + d, 8)).wait_send()

    def project(i):
        v_load(i).wait()
        return dot3((rtr[0], rtr[1]), split(v[:, pl.ds(mult(i, 256), 256)]))

    reduce_start(0, project)

    tt = split(t_ref[...])
    ttt = split(t_ref[...].T)

    @pl.loop(0, 4)
    def _(i):
        rows = pl.ds(mult(i, 512), 512)
        hi, lo = split(dot3(split(r[rows, :]), tt))
        rt[0, rows, :] = hi
        rt[1, rows, :] = lo
        hi, lo = split(dot3(ttt, (rtr[0, :, rows], rtr[1, :, rows])))
        rtt[0, :, rows] = hi
        rtt[1, :, rows] = lo

    for m in forwards:
        ag_arrived(m[0], m[1])
        ag(*m).start()

    def pa_copy(kk):
        cols = pl.ds(mult(k, 128), 128)
        return remote(pred, pfull.at[myrows, cols], pa_s.at[kk], pa_r.at[k], same_core(kk))

    def relay(kk):
        cols = pl.ds(mult(kk, 128), 128)
        return remote(
            pfull.at[myrows, cols], pfull.at[myrows, cols], pr_s.at[kk], pr_r.at[kk], partner
        )

    total = reduce_end(0)
    pred[...] = total
    pfull[myrows, pl.ds(mult(k, 128), 128)] = total
    for d in range(1, 8):
        pa_copy(lax.rem(k + d, 8)).start()
    relay(k).start()

    ag_arrived(zp, 0)
    ag_arrived(zp, 1)
    for m in zsends:
        ag(*m).start()

    for d in range(1, 8):
        kk = lax.rem(k + d, 8)
        remote(pred, pred, pa_s.at[0], pa_r.at[kk], partner).wait_recv()
        relay(kk).start()
    for kk in range(8):
        remote(pred, pred, pr_s.at[0], pr_r.at[kk], partner).wait_recv()

    for j in range(2):
        pbt[own, j * 128 : (j + 1) * 128] = pfull[j * 128 : (j + 1) * 128, OFF : OFF + 128].T[:BW, :]

    def pb_copy(nn):
        return remote(pbt.at[own], pbt.at[own], pb_s.at[nn], pb_r.at[n], narrow_peer(nn))

    for d in range(1, 8):
        pb_copy(lax.rem(n + d, 8)).start()

    def u_store(j):
        cols = pl.ds(mult(j, 256), 256)
        return pltpu.make_async_copy(v.at[pl.ds(0, ROWS), cols], u_hbm.at[:, cols], out_sem.at[j])

    @pl.loop(0, 4)
    def _(j):
        cols = pl.ds(mult(j, 256), 256)
        pj = split(pfull[:, cols])

        @pl.loop(0, 4)
        def _(i):
            rows = pl.ds(mult(i, 512), 512)
            u = v[rows, cols] - dot3((rt[0, rows, :], rt[1, rows, :]), pj)
            v[rows, cols] = u
            hi, lo = split(u)
            uu[0, rows, cols] = hi
            uu[1, rows, cols] = lo

        u_store(j).start()

    for m in zforwards:
        ag_arrived(m[0], m[1])
        ag(*m).start()
    for d in range(1, 8):
        nn = lax.rem(n + d, 8)
        remote(pbt.at[own], pbt.at[own], pb_s.at[0], pb_r.at[nn], partner).wait_recv()

    def f_copy(h, col):
        return remote(
            fsend.at[h], fo.at[:, pl.ds(pl.multiple_of(col, 128), 128)], f_s.at[h], f_r.at[h], partner
        )

    def fock(h, hb):
        @pl.loop(0, 4)
        def _(i):
            cols = pl.ds(mult(i, 512), 512)
            rows = pl.ds(mult(hb, 256), 256)
            p = split(pbt[rows, :])
            x = (vbt[rows, cols] - dot3(p, (rtt[0, :, cols], rtt[1, :, cols]))) * ep[:, cols]
            hi, lo = split(x)
            ub[0, :, cols] = hi
            ub[1, :, cols] = lo

        def compute(i):
            cols = pl.ds(mult(i, 256), 256)
            return dot3((ub[0], ub[1]), (uu[0, :, cols], uu[1, :, cols]))

        reduce_start(1 + h, compute)

    def fock_end(h, hb):
        red[...] = reduce_end(1 + h).T
        col = hb * 256 + c * 128
        fo[:, pl.ds(pl.multiple_of(col, 128), 128)] = red[pl.ds(mult(c, BW), BW), :]
        fsend[h] = red[pl.ds(mult(1 - c, BW), BW), :]
        f_copy(h, col).start()

    for d in (1, 2, 3):
        src = base + lax.rem(y + d, 4)
        for half in range(2):
            if (d == 3 and half == 0) or (d == 1 and half == 1):
                continue
            ag_arrived(src, half)
    fock(0, zh)
    for d in (1, 2, 3):
        src = zbase + lax.rem(y + d, 4)
        for half in range(2):
            if (d == 3 and half == 0) or (d == 1 and half == 1):
                continue
            ag_arrived(src, half)
    fock_end(0, zh)
    fock(1, 1 - zh)
    fock_end(1, 1 - zh)
    for h in range(2):
        f_copy(h, 0).wait_recv()
    f_ref[...] = fo[...]

    for h in range(2):
        f_copy(h, 0).wait_send()
    for m in sends + forwards + zsends + zforwards:
        ag(*m).wait_send()
    for st in range(3):
        reduce_drain(st)
    for d in range(1, 8):
        pa_copy(lax.rem(k + d, 8)).wait_send()
        pb_copy(lax.rem(n + d, 8)).wait_send()
    for kk in range(8):
        relay(kk).wait_send()
    for j in range(4):
        u_store(j).wait()


def on_device(vectors, reflectors, triangle, energies):
    vm = pl.BlockSpec(memory_space=pltpu.VMEM)
    hbm = pl.BlockSpec(memory_space=pl.ANY)
    dma = pltpu.SemaphoreType.DMA
    return pl.pallas_call(
        kernel,
        out_shape=(
            jax.ShapeDtypeStruct((ROWS, NC), F32),
            jax.ShapeDtypeStruct((BW, FB), F32),
        ),
        in_specs=[hbm, hbm, vm, vm],
        out_specs=(hbm, vm),
        scratch_shapes=[
            pltpu.VMEM((KP, NC), F32),
            pltpu.VMEM((KP, NB), F32),
            pltpu.VMEM((KP, 128), F32),
            pltpu.VMEM((2, NB, KP), BF16),
            pltpu.VMEM((2, KP, NB), BF16),
            pltpu.VMEM((2, NB, KP), BF16),
            pltpu.VMEM((2, KP, NC), BF16),
            pltpu.VMEM((FB, KP), F32),
            pltpu.VMEM((FB, NB), F32),
            pltpu.VMEM((1, KP), F32),
            pltpu.VMEM((3, 256, NC), F32),
            pltpu.VMEM((3, 128, NC), F32),
            pltpu.VMEM((3, 8, 128, 128), F32),
            pltpu.VMEM((128, 128), F32),
            pltpu.VMEM((NB, NC), F32),
            pltpu.VMEM((2, 256, KP), BF16),
            pltpu.VMEM((128, 128), F32),
            pltpu.VMEM((BW, FB), F32),
            pltpu.VMEM((2, BW, 128), F32),
            dma((6,)), dma((4,)), dma((14,)), dma((16,)), dma((12,)), dma((12,)),
            dma((24,)), dma((24,)), dma((8,)), dma((8,)), dma((8,)), dma((8,)),
            dma((8,)), dma((8,)), dma((2,)), dma((2,)),
        ],
        compiler_params=pltpu.CompilerParams(
            collective_id=0, has_side_effects=True, vmem_limit_bytes=56 * 2**20
        ),
        name="reflect_fock",
    )(vectors, reflectors, triangle, energies[None, :])


def solution(mesh):
    return jax.shard_map(
        on_device,
        mesh=mesh,
        in_specs=(P("wide", "narrow"), P("wide", None), P(), P("wide")),
        out_specs=(P("wide", "narrow"), P(("narrow", "wide"), None)),
        check_vma=False,
    )
```

```python
import functools

import jax
import jax.numpy as jnp
from jax import lax
from jax.experimental import pallas as pl
from jax.experimental.pallas import tpu as pltpu
from jax.sharding import PartitionSpec as P

MESH = pl.DeviceIdType.MESH
F32, BF16 = jnp.float32, jnp.bfloat16
ROWS, KP, NC, NB = 2000, 2048, 1024, 256
FB, OFF, BW = 512, 256, 64
M0, M1 = 320, 192


def dot(a, b):
    return jnp.dot(a, b, preferred_element_type=F32)


def split(x):
    hi = x.astype(BF16)
    return hi, (x - hi.astype(F32)).astype(BF16)


def dot3(a, b):
    return dot(a[0], b[0]) + dot(a[0], b[1]) + dot(a[1], b[0])


def mult(i, m):
    return pl.multiple_of(i * m, m)


def kernel(
    v_hbm, r_hbm, t_hbm, e_hbm, u_out, f_out,
    v, r, vb, t_ref, e_ref, rtr, rt, rtt, uu, vbt, pbt, ep, part0, part1, part2, xrecv0, xrecv1, xrecv2,
    rsr0, rsr1, rsr2, pfull, ub, fl, fg, ft,
    ld_sem, ag_s, ag_r, xs, xr, rs_s, rs_r, pa_s, pa_r, pr_s, pr_r, pb_s, pb_r, f_s, f_r,
):
    w, n = lax.axis_index("wide"), lax.axis_index("narrow")
    c, k = lax.rem(w, 2), w // 2
    y, zh = lax.rem(n, 4), n // 4
    partner = (w + 1 - 2 * c, n)
    yp, ym = zh * 4 + lax.rem(y + 1, 4), zh * 4 + lax.rem(y + 3, 4)
    base = zh * 4
    zbase = (1 - zh) * 4

    def same_core(kk):
        return (2 * kk + c, n)

    def narrow_peer(nn):
        return (w, nn)

    def remote(src, dst, s, rsem, to):
        return pltpu.make_async_remote_copy(
            src_ref=src, dst_ref=dst, send_sem=s, recv_sem=rsem, device_id=to, device_id_type=MESH
        )

    kk0 = k // 2

    def order(s):
        return lax.rem(kk0 + 1 + s, 4)

    vb_load = pltpu.make_async_copy(v_hbm.at[:, pl.ds(OFF, 128)], vb.at[pl.ds(0, ROWS)], ld_sem.at[0])
    r_load = pltpu.make_async_copy(r_hbm, r.at[pl.ds(0, ROWS)], ld_sem.at[1])

    def v_load(i):
        cols = pl.ds(mult(i, 256), 256)
        return pltpu.make_async_copy(v_hbm.at[:, cols], v.at[pl.ds(0, ROWS), cols], ld_sem.at[2 + i])

    t_load = pltpu.make_async_copy(t_hbm, t_ref, ld_sem.at[6])
    e_load = pltpu.make_async_copy(e_hbm, e_ref, ld_sem.at[7])
    vb_load.start()
    r_load.start()
    for s in range(4):
        v_load(order(s)).start()
    t_load.start()
    e_load.start()

    barrier = pltpu.get_barrier_semaphore()
    pl.semaphore_signal(barrier, inc=1, device_id=partner, device_id_type=MESH)
    for d in range(1, 8):
        pl.semaphore_signal(barrier, inc=1, device_id=same_core(lax.rem(k + d, 8)), device_id_type=MESH)
        pl.semaphore_signal(barrier, inc=1, device_id=narrow_peer(lax.rem(n + d, 8)), device_id_type=MESH)

    vb[ROWS:, :] = jnp.zeros((KP - ROWS, 128), F32)
    r[ROWS:, :] = jnp.zeros((KP - ROWS, NB), F32)
    v[ROWS:, :] = jnp.zeros((KP - ROWS, NC), F32)

    vb_load.wait()
    own = pl.ds(mult(n, BW), BW)
    for i in range(KP // 128):
        vbt[own, i * 128 : (i + 1) * 128] = vb[i * 128 : (i + 1) * 128, :].T[:BW, :]
    pl.semaphore_wait(barrier, 15)

    def ag(src_n, o, cnt, to, slot):
        rows = pl.ds(mult(src_n * 8 + o, 8), 8 * cnt)
        return remote(vbt.at[rows], vbt.at[rows], ag_s.at[slot], ag_r.at[src_n * 8 + o], narrow_peer(to))

    def arrived(src_n, o, cnt):
        ag(src_n, o, cnt, yp, 0).wait_recv()

    zp = zbase + y
    zyp, zym = zbase + lax.rem(y + 1, 4), zbase + lax.rem(y + 3, 4)
    y2, zy2 = base + lax.rem(y + 2, 4), zbase + lax.rem(y + 2, 4)
    z_sends = [(n, 2 * q, 2, zp, q) for q in range(4)]
    zx_sends = [(ym, 6, 2, zp, 4), (yp, 6, 2, zp, 5), (y2, 6, 2, zp, 6)]
    y_sends = [(n, 0, 4, yp, 7), (n, 0, 4, ym, 8), (n, 4, 4, yp, 9), (n, 4, 4, ym, 10)]
    y_fwds = [(ym, 0, 2, yp, 11), (yp, 2, 2, ym, 12), (ym, 4, 2, yp, 13), (yp, 6, 2, ym, 14)]
    p_sends = [(zp, 0, 4, yp, 15), (zp, 0, 4, ym, 16), (zp, 4, 2, yp, 17), (zp, 4, 2, ym, 18)]
    p_fwds = [(zym, 0, 2, yp, 19), (zyp, 2, 2, ym, 20), (zym, 4, 1, yp, 21), (zyp, 5, 1, ym, 22)]
    every = z_sends + zx_sends + y_sends + y_fwds + p_sends + p_fwds

    def go(messages):
        for m in messages:
            ag(*m).start()

    go(z_sends[:1] + y_sends)

    r_load.wait()

    @pl.loop(0, 4)
    def _(i):
        rows = pl.ds(mult(i, 512), 512)
        hi, lo = split(r[rows, :])
        rtr[0, :, rows] = hi.T
        rtr[1, :, rows] = lo.T

    part, xrecv, rsr = (part0, part1, part2), (xrecv0, xrecv1, xrecv2), (rsr0, rsr1, rsr2)
    half_rows = (128, M0 // 2, M1 // 2)
    myrows = pl.ds(mult(c, 128), 128)
    hisrows = pl.ds(mult(1 - c, 128), 128)

    def mine(st):
        return pl.ds(mult(c, half_rows[st]), half_rows[st])

    def his(st):
        return pl.ds(mult(1 - c, half_rows[st]), half_rows[st])

    def x_copy(st, i):
        cols = pl.ds(mult(i, 256), 256)
        return remote(
            part[st].at[his(st), cols], xrecv[st].at[:, cols], xs.at[st * 4 + i], xr.at[st * 4 + i], partner
        )

    def rs_copy(st, kk):
        return remote(
            part[st].at[mine(st), pl.ds(mult(kk, 128), 128)], rsr[st].at[k], rs_s.at[st * 8 + kk],
            rs_r.at[st * 8 + k], same_core(kk),
        )

    def finish(st, i):
        cols = pl.ds(mult(i, 256), 256)
        x_copy(st, i).wait_recv()
        part[st][mine(st), cols] = part[st][mine(st), cols] + xrecv[st][:, cols]
        for t in range(2):
            kk = 2 * i + t

            @pl.when(kk != k)
            def _():
                rs_copy(st, kk).start()

    def reduce_start(st, compute, hooks=()):
        @pl.loop(0, 4)
        def _(s):
            i = order(s)
            part[st][:, pl.ds(mult(i, 256), 256)] = compute(i)
            x_copy(st, i).start()

            @pl.when(s >= 1)
            def _():
                finish(st, order(s - 1))

            for at, hook in hooks:

                @pl.when(s == at)
                def _():
                    hook()

    def reduce_end(st):
        total = part[st][mine(st), pl.ds(mult(k, 128), 128)]
        for d in range(1, 8):
            kk = lax.rem(k + d, 8)
            remote(rsr[st].at[kk], rsr[st].at[kk], rs_s.at[st * 8], rs_r.at[st * 8 + kk], partner).wait_recv()
            total = total + rsr[st][kk]
        return total

    def reduce_drain(st):
        for i in range(4):
            x_copy(st, i).wait_send()
        for d in range(1, 8):
            rs_copy(st, lax.rem(k + d, 8)).wait_send()

    def project(i):
        v_load(i).wait()
        return dot3((rtr[0], rtr[1]), split(v[:, pl.ds(mult(i, 256), 256)]))

    reduce_start(0, project)

    t_load.wait()
    e_load.wait()
    ep[...] = jnp.zeros((1, KP), F32)
    ep[:, :ROWS] = e_ref[...]
    tt = split(t_ref[...])
    ttt = split(t_ref[...].T)

    @pl.loop(0, 2)
    def _(i):
        rows = pl.ds(mult(i, 1024), 1024)
        hi, lo = split(dot3(split(r[rows, :]), tt))
        rt[0, rows, :] = hi
        rt[1, rows, :] = lo

        @pl.when(i == 0)
        def _():
            finish(0, order(3))
            go(z_sends[1:2])

    @pl.loop(0, 2)
    def _(i):
        rows = pl.ds(mult(i, 1024), 1024)
        hi, lo = split(dot3(ttt, (rtr[0, :, rows], rtr[1, :, rows])))
        rtt[0:256, rows] = hi
        rtt[256:512, rows] = lo
        rtt[512:768, rows] = hi

    arrived(ym, 0, 4)
    arrived(yp, 0, 4)
    go(y_fwds[:2])

    x, zl = lax.rem(k, 4), k // 4
    kz = (1 - zl) * 4 + x

    def slice_copy(src_k, to_k, slot):
        cols = pl.ds(mult(src_k, 128), 128)
        return remote(
            pfull.at[myrows, cols], pfull.at[myrows, cols], pa_s.at[slot], pa_r.at[src_k], same_core(to_k)
        )

    x_peers = [zl * 4 + lax.rem(x + d, 4) for d in (1, 3, 2)]
    slices = [(k, kz, 0)] + [(k, kx, 1 + d) for d, kx in enumerate(x_peers)]
    z_slices = [(kz, kx, 4 + d) for d, kx in enumerate(x_peers)]

    def slice_here(kk):
        slice_copy(kk, kz, 0).wait_recv()

    def relay(kk):
        cols = pl.ds(mult(kk, 128), 128)
        return remote(
            pfull.at[myrows, cols], pfull.at[myrows, cols], pr_s.at[kk], pr_r.at[kk], partner
        )

    total = reduce_end(0)
    pfull[myrows, pl.ds(mult(k, 128), 128)] = total
    for m in slices:
        slice_copy(*m).start()
    relay(k).start()
    go(z_sends[2:])
    arrived(ym, 4, 4)
    arrived(yp, 4, 4)
    go(y_fwds[2:])
    slice_here(kz)
    for m in z_slices:
        slice_copy(*m).start()
    relay(kz).start()
    arrived(zp, 0, 2)
    arrived(zp, 2, 2)
    go(p_sends[:2])
    for kx in x_peers:
        slice_here(kx)
        relay(kx).start()
    def relay_in(kk):
        cols = pl.ds(mult(kk, 128), 128)
        return remote(pfull.at[hisrows, cols], pfull.at[hisrows, cols], pr_s.at[0], pr_r.at[kk], partner)

    def slice_arrived(kk):
        relay_in(kk).wait_recv()

    def pb_rows(nn, cc):
        return pbt.at[pl.ds(mult(2 * nn + cc, 32), 32)]

    def pb_copy(nn):
        return remote(pb_rows(n, c), pb_rows(n, c), pb_s.at[nn], pb_r.at[n], narrow_peer(nn))

    def pb_in(nn):
        return remote(pb_rows(nn, c), pb_rows(nn, c), pb_s.at[0], pb_r.at[nn], partner)

    def pb_relay(nn, cc):
        return remote(pb_rows(nn, cc), pb_rows(nn, cc), pb_s.at[8 + nn], pb_r.at[8 + nn], partner)

    peers = [base + lax.rem(y + d, 4) for d in (1, 3, 2)] + [zp, zyp, zym, zy2]

    def pb_send():
        for j in range(2):
            pbt[own, j * 128 : (j + 1) * 128] = pfull[j * 128 : (j + 1) * 128, OFF : OFF + 128].T[:BW, :]
        for nn in peers:
            pb_copy(nn).start()

    uu[0, ROWS:, :] = jnp.zeros((KP - ROWS, NC), BF16)
    uu[1, ROWS:, :] = jnp.zeros((KP - ROWS, NC), BF16)

    def update(zz):
        @pl.loop(0, 2)
        def _(j):
            cols = pl.ds(mult(2 * zz + j, 256), 256)
            p = split(pfull[:, cols])
            u = v[:ROWS, cols] - dot3((rt[0, :ROWS, :], rt[1, :ROWS, :]), p)
            u_out[:, cols] = u
            hi, lo = split(u)
            uu[0, :ROWS, cols] = hi
            uu[1, :ROWS, cols] = lo

    for kx in [k] + x_peers:
        slice_arrived(kx)

    @pl.when(zl == 0)
    def _():
        pb_send()

    update(zl)
    z_peers = [(1 - zl) * 4 + lax.rem(x + d, 4) for d in (1, 3, 2)]
    for kx in z_peers:
        slice_here(kx)
        relay(kx).start()
    for kx in [kz] + z_peers:
        slice_arrived(kx)

    @pl.when(zl == 1)
    def _():
        pb_send()

    arrived(zp, 4, 2)
    go(p_sends[2:])
    arrived(y2, 6, 2)
    go(zx_sends)
    update(1 - zl)
    arrived(zym, 0, 4)
    arrived(zyp, 0, 4)
    go(p_fwds[:2])
    for nn in peers:
        pb_in(nn).wait_recv()
        pb_relay(nn, c).start()
    for nn in peers:
        pb_relay(nn, 1 - c).wait_recv()

    blocks = [base + d for d in range(4)] + [zp, zyp, zy2, zym]

    def f_copy(h):
        first = h * M0
        rows = pl.ds(pl.multiple_of(first + c * half_rows[1 + h], 32), half_rows[1 + h])
        return remote(fl.at[rows], fl.at[rows], f_s.at[h], f_r.at[h], partner)

    def fock(h, hooks=()):
        srcs = [pl.ds(mult(nn, BW), BW) for nn in (blocks[:5] if h == 0 else blocks[5:])]
        if h == 0:
            srcs = [pl.ds(mult(zh, 4 * BW), 4 * BW)] + srcs[4:]
        hi, lo = split(jnp.concatenate([pbt[src, :] for src in srcs], axis=0))
        p = jnp.concatenate([hi, hi, lo], axis=1)

        @pl.loop(0, 2)
        def _(i):
            cols = pl.ds(mult(i, 1024), 1024)
            vv = jnp.concatenate([vbt[src, cols] for src in srcs], axis=0)
            hi, lo = split((vv - dot(p, rtt[:, cols])) * ep[:, cols])
            ub[0, : hi.shape[0], cols] = hi
            ub[1, : hi.shape[0], cols] = lo

        m = M0 if h == 0 else M1

        def compute(i):
            cols = pl.ds(mult(i, 256), 256)
            return dot3((ub[0, :m], ub[1, :m]), (uu[0, :, cols], uu[1, :, cols]))

        reduce_start(1 + h, compute, hooks)

    def fock_end(h):
        first = h * M0
        rows = pl.ds(pl.multiple_of(first + c * half_rows[1 + h], 32), half_rows[1 + h])
        fl[rows, :] = reduce_end(1 + h)
        f_copy(h).start()

    for o in (0, 2, 4):
        arrived(y2, o, 2)
    arrived(zp, 6, 2)

    def pass_last():
        arrived(zym, 4, 2)
        arrived(zyp, 4, 2)
        go(p_fwds[2:])

    fock(0, [(0, pass_last)])
    arrived(zym, 6, 2)
    arrived(zyp, 6, 2)
    for o, cnt in ((0, 2), (2, 2), (4, 1), (5, 1), (6, 2)):
        arrived(zy2, o, cnt)
    fock(1, [(0, lambda: finish(1, order(3)))])
    finish(2, order(3))
    fock_end(0)
    fock_end(1)
    def f_in(h):
        rows = pl.ds(pl.multiple_of(h * M0 + (1 - c) * half_rows[1 + h], 32), half_rows[1 + h])
        return remote(fl.at[rows], fl.at[rows], f_s.at[h], f_r.at[h], partner)

    for h in range(2):
        f_in(h).wait_recv()
    for at, nn in enumerate(blocks):
        fg[pl.ds(mult(nn, BW), BW), :] = fl[at * BW : (at + 1) * BW, :]
    ft[...] = fg[...].T
    f_out[...] = ft[pl.ds(mult(c, BW), BW), :]

    for h in range(2):
        f_copy(h).wait_send()
    for m in every:
        ag(*m).wait_send()
    for st in range(3):
        reduce_drain(st)
    for m in slices + z_slices:
        slice_copy(*m).wait_send()
    for nn in peers:
        pb_copy(nn).wait_send()
        pb_relay(nn, c).wait_send()
    for kk in range(8):
        relay(kk).wait_send()


def on_device(vectors, reflectors, triangle, energies):
    vm = pl.BlockSpec(memory_space=pltpu.VMEM)
    hbm = pl.BlockSpec(memory_space=pl.ANY)
    dma = pltpu.SemaphoreType.DMA
    return pl.pallas_call(
        kernel,
        out_shape=(
            pltpu.VMEM((ROWS, NC), F32),
            pltpu.VMEM((BW, FB), F32),
        ),
        in_specs=[hbm, hbm, hbm, hbm],
        out_specs=(vm, vm),
        scratch_shapes=[
            pltpu.VMEM((KP, NC), F32),
            pltpu.VMEM((KP, NB), F32),
            pltpu.VMEM((KP, 128), F32),
            pltpu.VMEM((NB, NB), F32),
            pltpu.VMEM((1, ROWS), F32),
            pltpu.VMEM((2, NB, KP), BF16),
            pltpu.VMEM((2, KP, NB), BF16),
            pltpu.VMEM((3 * NB, KP), BF16),
            pltpu.VMEM((2, KP, NC), BF16),
            pltpu.VMEM((FB, KP), F32),
            pltpu.VMEM((FB, NB), F32),
            pltpu.VMEM((1, KP), F32),
            pltpu.VMEM((NB, NC), F32),
            pltpu.VMEM((M0, NC), F32),
            pltpu.VMEM((M1, NC), F32),
            pltpu.VMEM((128, NC), F32),
            pltpu.VMEM((M0 // 2, NC), F32),
            pltpu.VMEM((M1 // 2, NC), F32),
            pltpu.VMEM((8, 128, 128), F32),
            pltpu.VMEM((8, M0 // 2, 128), F32),
            pltpu.VMEM((8, M1 // 2, 128), F32),
            pltpu.VMEM((NB, NC), F32),
            pltpu.VMEM((2, M0, KP), BF16),
            pltpu.VMEM((FB, 128), F32),
            pltpu.VMEM((FB, 128), F32),
            pltpu.VMEM((128, FB), F32),
            dma((8,)), dma((23,)), dma((64,)), dma((12,)), dma((12,)),
            dma((24,)), dma((24,)), dma((8,)), dma((8,)), dma((8,)), dma((8,)),
            dma((16,)), dma((16,)), dma((2,)), dma((2,)),
        ],
        compiler_params=pltpu.CompilerParams(
            collective_id=0, has_side_effects=True, vmem_limit_bytes=50 * 2**20
        ),
        name="reflect_fock",
    )(vectors, reflectors, triangle, energies[None, :])


def solution(mesh):
    return jax.shard_map(
        on_device,
        mesh=mesh,
        in_specs=(P("wide", "narrow"), P("wide", None), P(), P("wide")),
        out_specs=(P("wide", "narrow"), P(("narrow", "wide"), None)),
        check_vma=False,
    )
```

```python
import functools

import jax
import jax.numpy as jnp
from jax import lax
from jax.experimental import pallas as pl
from jax.experimental.pallas import tpu as pltpu
from jax.sharding import PartitionSpec as P

MESH = pl.DeviceIdType.MESH
F32, BF16 = jnp.float32, jnp.bfloat16
ROWS, KP, NC, NB = 2000, 2048, 1024, 256
FB, OFF, BW = 512, 256, 64
PARTS = (256, 192, 64)
KB = OFF // 128


def dot(a, b):
    return jnp.dot(a, b, preferred_element_type=F32)


def split(x):
    hi = x.astype(BF16)
    return hi, (x - hi.astype(F32)).astype(BF16)


def dot3(a, b):
    return dot(a[0], b[0]) + dot(a[0], b[1]) + dot(a[1], b[0])


def mult(i, m):
    return pl.multiple_of(i * m, m)


def kernel(
    v_hbm, r_hbm, t_hbm, e_hbm, u_out, f_out,
    v, r, vb, t_ref, e_ref, rtr, rt, yt, a3, a4, bb, uu, vbt, pbt, ep, part0, part1, part2, part3, xrecv0, xrecv1, xrecv2,
    xrecv3, rsr0, rsr1, rsr2, rsr3, pfull, ub, fl, fg, ft,
    ld_sem, ag_s, ag_r, xs, xr, rs_s, rs_r, pa_s, pa_r, pr_s, pr_r, pb_s, pb_r, f_s, f_r,
):
    w, n = lax.axis_index("wide"), lax.axis_index("narrow")
    c, k = lax.rem(w, 2), w // 2
    y, zh = lax.rem(n, 4), n // 4
    partner = (w + 1 - 2 * c, n)
    yp, ym = zh * 4 + lax.rem(y + 1, 4), zh * 4 + lax.rem(y + 3, 4)
    base = zh * 4
    zbase = (1 - zh) * 4

    def same_core(kk):
        return (2 * kk + c, n)

    def narrow_peer(nn):
        return (w, nn)

    def remote(src, dst, s, rsem, to):
        return pltpu.make_async_remote_copy(
            src_ref=src, dst_ref=dst, send_sem=s, recv_sem=rsem, device_id=to, device_id_type=MESH
        )

    kk0 = k // 2

    def order(s):
        t1, t0 = (3 - s) // 2, lax.rem(3 - s, 2)
        a, b = kk0 // 2, lax.rem(kk0, 2)
        return 2 * (a + t1 - 2 * a * t1) + b + t0 - 2 * b * t0

    vb_load = pltpu.make_async_copy(v_hbm.at[:, pl.ds(OFF, 128)], vb.at[pl.ds(0, ROWS)], ld_sem.at[0])
    r_load = pltpu.make_async_copy(r_hbm, r.at[pl.ds(0, ROWS)], ld_sem.at[1])

    def v_load(i):
        cols = pl.ds(mult(i, 256), 256)
        return pltpu.make_async_copy(v_hbm.at[:, cols], v.at[pl.ds(0, ROWS), cols], ld_sem.at[2 + i])

    t_load = pltpu.make_async_copy(t_hbm, t_ref, ld_sem.at[6])
    e_load = pltpu.make_async_copy(e_hbm, e_ref, ld_sem.at[7])
    vb_load.start()
    r_load.start()
    for s in range(4):
        v_load(order(s)).start()
    t_load.start()
    e_load.start()

    barrier = pltpu.get_barrier_semaphore()
    pl.semaphore_signal(barrier, inc=1, device_id=partner, device_id_type=MESH)
    for d in range(1, 8):
        pl.semaphore_signal(barrier, inc=1, device_id=same_core(lax.rem(k + d, 8)), device_id_type=MESH)
        pl.semaphore_signal(barrier, inc=1, device_id=narrow_peer(lax.rem(n + d, 8)), device_id_type=MESH)

    vb[ROWS:, :] = jnp.zeros((KP - ROWS, 128), F32)
    r[ROWS:, :] = jnp.zeros((KP - ROWS, NB), F32)
    v[ROWS:, :] = jnp.zeros((KP - ROWS, NC), F32)

    vb_load.wait()
    own = pl.ds(mult(n, BW), BW)
    for i in range(KP // 128):
        vbt[own, i * 128 : (i + 1) * 128] = vb[i * 128 : (i + 1) * 128, :].T[:BW, :]
    pl.semaphore_wait(barrier, 15)

    def ag(src_n, o, cnt, to, slot):
        rows = pl.ds(mult(src_n * 8 + o, 8), 8 * cnt)
        return remote(vbt.at[rows], vbt.at[rows], ag_s.at[slot], ag_r.at[src_n * 8 + o], narrow_peer(to))

    def arrived(src_n, o, cnt):
        ag(src_n, o, cnt, yp, 0).wait_recv()

    zp = zbase + y
    zyp, zym = zbase + lax.rem(y + 1, 4), zbase + lax.rem(y + 3, 4)
    y2, zy2 = base + lax.rem(y + 2, 4), zbase + lax.rem(y + 2, 4)
    z_sends = [(n, 2 * q, 2, zp, q) for q in range(4)]
    zx_sends = [(ym, 7, 1, zp, 4), (yp, 7, 1, zp, 5), (y2, 7, 1, zp, 6)]
    y_sends = [(n, 0, 4, yp, 7), (n, 0, 4, ym, 8), (n, 4, 4, yp, 9), (n, 4, 4, ym, 10)]
    y_fwds = [(ym, 0, 2, yp, 11), (yp, 2, 2, ym, 12), (ym, 4, 2, yp, 13), (yp, 6, 2, ym, 14)]
    p_sends = [
        (zp, 0, 2, yp, 15), (zp, 0, 2, ym, 16), (zp, 2, 2, yp, 17), (zp, 2, 2, ym, 18), (zp, 4, 2, yp, 19),
        (zp, 4, 2, ym, 20), (zp, 6, 1, yp, 25), (zp, 6, 1, ym, 26),
    ]
    p_fwds = [(zym, 0, 2, yp, 21), (zyp, 2, 2, ym, 22), (zym, 4, 1, yp, 23), (zyp, 5, 1, ym, 24), (zym, 6, 1, yp, 27)]
    every = z_sends + zx_sends + y_sends + y_fwds + p_sends + p_fwds

    def go(messages):
        for m in messages:
            ag(*m).start()

    go(z_sends[:1] + y_sends)

    r_load.wait()

    @pl.loop(0, 4)
    def _(i):
        rows = pl.ds(mult(i, 512), 512)
        hi, lo = split(r[rows, :])
        rtr[0, :, rows] = hi.T
        rtr[1, :, rows] = lo.T

    part, xrecv = (part0, part1, part2, part3), (xrecv0, xrecv1, xrecv2, xrecv3)
    rsr = (rsr0, rsr1, rsr2, rsr3)
    half_rows = (128,) + tuple(m // 2 for m in PARTS)
    myrows = pl.ds(mult(c, 128), 128)
    hisrows = pl.ds(mult(1 - c, 128), 128)

    def mine(st):
        return pl.ds(mult(c, half_rows[st]), half_rows[st])

    def his(st):
        return pl.ds(mult(1 - c, half_rows[st]), half_rows[st])

    def x_copy(st, i):
        cols = pl.ds(mult(i, 256), 256)
        return remote(
            part[st].at[his(st), cols], xrecv[st].at[:, cols], xs.at[st * 4 + i], xr.at[st * 4 + i], partner
        )

    def rs_copy(st, kk):
        return remote(
            part[st].at[mine(st), pl.ds(mult(kk, 128), 128)], rsr[st].at[k], rs_s.at[st * 8 + kk],
            rs_r.at[st * 8 + k], same_core(kk),
        )

    def finish(st, i):
        cols = pl.ds(mult(i, 256), 256)
        x_copy(st, i).wait_recv()
        part[st][mine(st), cols] = part[st][mine(st), cols] + xrecv[st][:, cols]
        for t in range(2):
            kk = 2 * i + t

            @pl.when(kk != k)
            def _():
                rs_copy(st, kk).start()

    def reduce_start(st, compute, hooks=(), lag=1):
        @pl.loop(0, 4)
        def _(s):
            i = order(s)
            part[st][:, pl.ds(mult(i, 256), 256)] = compute(i)
            x_copy(st, i).start()

            @pl.when(s >= lag)
            def _():
                finish(st, order(s - lag))

            for at, hook in hooks:

                @pl.when(s == at)
                def _():
                    hook()

    def reduce_end(st):
        total = part[st][mine(st), pl.ds(mult(k, 128), 128)]
        for d in range(1, 8):
            kk = lax.rem(k + d, 8)
            remote(rsr[st].at[kk], rsr[st].at[kk], rs_s.at[st * 8], rs_r.at[st * 8 + kk], partner).wait_recv()
            total = total + rsr[st][kk]
        return total

    def reduce_drain(st):
        for i in range(4):
            x_copy(st, i).wait_send()
        for d in range(1, 8):
            rs_copy(st, lax.rem(k + d, 8)).wait_send()

    def project(i):
        v_load(i).wait()
        cols = pl.ds(mult(i, 256), 256)
        hi, lo = split(v[:, cols])
        uu[0, :, cols] = hi
        uu[1, :, cols] = lo
        return dot3((rtr[0], rtr[1]), (hi, lo))

    reduce_start(0, project)

    t_load.wait()
    e_load.wait()
    ep[...] = jnp.zeros((1, KP), F32)
    ep[:, :ROWS] = e_ref[...]
    tt = split(t_ref[...])
    ttt = split(t_ref[...].T)

    @pl.loop(0, 2)
    def _(i):
        rows = pl.ds(mult(i, 1024), 1024)
        hi, lo = split(dot3(split(r[rows, :]), tt))
        rt[0, rows, :] = hi
        rt[1, rows, :] = lo

        @pl.when(i == 0)
        def _():
            finish(0, order(3))
            go(z_sends[1:2])

    @pl.loop(0, 2)
    def _(i):
        rows = pl.ds(mult(i, 1024), 1024)
        hi, lo = split(dot3(ttt, (rtr[0, :, rows], rtr[1, :, rows])) * ep[:, rows])
        yt[0, :, rows] = hi
        yt[1, :, rows] = lo

    x, zl = lax.rem(k, 4), k // 4
    kz = (1 - zl) * 4 + x

    def slice_copy(src_k, to_k, slot):
        cols = pl.ds(mult(src_k, 128), 128)
        return remote(
            pfull.at[myrows, cols], pfull.at[myrows, cols], pa_s.at[slot], pa_r.at[src_k], same_core(to_k)
        )

    x_peers = [zl * 4 + lax.rem(x + d, 4) for d in (1, 3, 2)]
    slices = [(k, kz, 0)] + [(k, kx, 1 + d) for d, kx in enumerate(x_peers)]
    z_slices = [(kz, kx, 4 + d) for d, kx in enumerate(x_peers)]

    def slice_here(kk):
        slice_copy(kk, kz, 0).wait_recv()

    def relay(kk):
        cols = pl.ds(mult(kk, 128), 128)
        return remote(
            pfull.at[myrows, cols], pfull.at[myrows, cols], pr_s.at[kk], pr_r.at[kk], partner
        )

    def own_slice():
        pfull[myrows, pl.ds(mult(k, 128), 128)] = reduce_end(0)
        for m in slices:
            slice_copy(*m).start()

        relay(k).start()
        go(z_sends[2:])

    @pl.loop(0, 4)
    def _(i):
        cols = pl.ds(mult(i, 256), 256)
        a3[:, cols] = dot3((yt[0], yt[1]), (uu[0, :, cols], uu[1, :, cols]))

        @pl.when(i == 1)
        def _():
            arrived(ym, 0, 4)
            arrived(yp, 0, 4)
            go(y_fwds[:2])
            own_slice()

        @pl.when(i == 2)
        def _():
            arrived(ym, 4, 4)
            arrived(yp, 4, 4)
            go(y_fwds[2:])

    slice_here(kz)
    for m in z_slices:
        slice_copy(*m).start()
    relay(kz).start()
    arrived(zp, 0, 2)
    go(p_sends[:2])
    for kx in x_peers:
        slice_here(kx)
        relay(kx).start()

    def relay_in(kk):
        cols = pl.ds(mult(kk, 128), 128)
        return remote(pfull.at[hisrows, cols], pfull.at[hisrows, cols], pr_s.at[0], pr_r.at[kk], partner)

    def slice_arrived(kk):
        relay_in(kk).wait_recv()

    def pb_rows(nn, cc):
        return pbt.at[pl.ds(mult(2 * nn + cc, 32), 32)]

    def pb_copy(nn):
        return remote(pb_rows(n, c), pb_rows(n, c), pb_s.at[nn], pb_r.at[n], narrow_peer(nn))

    def pb_in(nn):
        return remote(pb_rows(nn, c), pb_rows(nn, c), pb_s.at[0], pb_r.at[nn], partner)

    def pb_relay(nn, cc):
        return remote(pb_rows(nn, cc), pb_rows(nn, cc), pb_s.at[8 + nn], pb_r.at[8 + nn], partner)

    peers = [base + lax.rem(y + d, 4) for d in (1, 3, 2)] + [zp, zyp, zym, zy2]

    def pb_send():
        for j in range(2):
            pbt[own, j * 128 : (j + 1) * 128] = pfull[j * 128 : (j + 1) * 128, OFF : OFF + 128].T[:BW, :]
        for nn in peers:
            pb_copy(nn).start()

    blocks = [base + d for d in range(4)] + [zp, zyp, zym, zy2]
    firsts = (0, PARTS[0], PARTS[0] + PARTS[1])

    def sources(h):
        if h == 0:
            return [pl.ds(mult(zh, 4 * BW), 4 * BW)]
        return [pl.ds(mult(nn, BW), BW) for nn in (blocks[4:7] if h == 1 else blocks[7:])]

    def scaled(h):
        at, m = 0, PARTS[h]
        for src in sources(h):
            hi, lo = split(vbt[src, :] * ep[...])
            ub[at : at + hi.shape[0], :] = hi
            ub[m + at : m + at + hi.shape[0], :] = lo
            at += hi.shape[0]

    hi, lo = split(dot3((yt[0], yt[1]), (rt[0], rt[1])))
    a4[0] = hi
    a4[1] = lo
    for kx in [k] + x_peers:
        slice_arrived(kx)

    @pl.when((zl == 1) & (kz != KB))
    def _():
        slice_here(KB)
        relay(KB).start()

    def block_columns():
        @pl.when(zl == 1)
        def _():
            slice_arrived(KB)

        pb_send()
        arrived(zp, 2, 2)
        go(p_sends[2:4] + zx_sends[:2])
        arrived(zp, 4, 2)
        go(p_sends[4:6])

    z_peers = [(1 - zl) * 4 + lax.rem(x + d, 4) for d in (1, 3, 2)]

    def pb_pass(some):
        for nn in some:
            pb_in(nn).wait_recv()
            pb_relay(nn, c).start()

    def others():
        for kx in z_peers:

            @pl.when((zl == 0) | (kx != KB))
            def _():
                slice_here(kx)
                relay(kx).start()

        for o in (0, 2, 4, 6):
            arrived(y2, o, 2)
        go(zx_sends[2:])
        scaled(0)
        arrived(zp, 6, 2)
        go(p_sends[6:])
        arrived(zym, 0, 2)
        go(p_fwds[:1])
        for kx in [kz] + z_peers:

            @pl.when((zl == 0) | (kx != KB))
            def _():
                slice_arrived(kx)

    @pl.loop(0, 4)
    def _(s):
        cols = pl.ds(mult(lax.rem(2 * zl + s, 4), 256), 256)
        p = split(pfull[:, cols])
        u = v[:ROWS, cols] - dot3((rt[0, :ROWS, :], rt[1, :ROWS, :]), p)
        u_out[:, cols] = u
        hi, lo = split(u)
        uu[0, :ROWS, cols] = hi
        uu[1, :ROWS, cols] = lo
        hi, lo = split(a3[:, cols] - dot3((a4[0], a4[1]), p))
        bb[0, :, cols] = hi
        bb[1, :, cols] = lo

        @pl.when(s == 0)
        def _():
            block_columns()

        @pl.when(s == 1)
        def _():
            others()

        @pl.when(s == 2)
        def _():
            pb_pass(peers[:3])

    def f_rows(h, cc):
        rows = pl.ds(pl.multiple_of(firsts[h] + cc * half_rows[1 + h], 32), half_rows[1 + h])
        return fl.at[rows]

    def f_copy(h, cc):
        return remote(f_rows(h, cc), f_rows(h, cc), f_s.at[h], f_r.at[h], partner)

    def pb_part(h, i):
        cols = pl.ds(mult(i, 256), 256)
        return dot3(split(jnp.concatenate([pbt[src, :] for src in sources(h)], axis=0)), (bb[0, :, cols], bb[1, :, cols]))

    def main_part(h, i):
        m = PARTS[h]
        cols = pl.ds(mult(i, 256), 256)
        if h < 2:
            return dot3((ub[:m], ub[m : 2 * m]), (uu[0, :, cols], uu[1, :, cols]))
        both = dot(ub[: 2 * m], uu[0, :, cols])
        return both[:m] + both[m:] + dot(ub[:m], uu[1, :, cols])

    def pass_some():
        arrived(zyp, 2, 2)
        go(p_fwds[1:2])
        pb_pass(peers[3:])

    def pass_last():
        arrived(zym, 4, 2)
        arrived(zyp, 4, 2)
        go(p_fwds[2:4])

    def fock_end(h):
        f_rows(h, c)[...] = reduce_end(1 + h)
        f_copy(h, c).start()

    for nn in peers[:3]:
        pb_relay(nn, 1 - c).wait_recv()
    reduce_start(1, lambda i: main_part(0, i) - pb_part(0, i), [(1, pass_some), (3, pass_last)])
    arrived(zym, 6, 1)
    go(p_fwds[4:])
    for nn in peers[3:]:
        pb_relay(nn, 1 - c).wait_recv()
    for src, o, cnt in ((zym, 2, 2), (zym, 7, 1), (zyp, 0, 2), (zyp, 6, 1), (zyp, 7, 1)):
        arrived(src, o, cnt)
    scaled(1)
    reduce_start(2, lambda i: main_part(1, i) - pb_part(1, i), [(0, lambda: finish(1, order(3)))])
    finish(2, order(3))
    for o, cnt in ((0, 2), (2, 2), (4, 1), (5, 1), (6, 1), (7, 1)):
        arrived(zy2, o, cnt)
    scaled(2)
    reduce_start(3, lambda i: main_part(2, i) - pb_part(2, i), lag=2)
    finish(3, order(2))
    finish(3, order(3))
    fock_end(0)
    fock_end(1)
    fock_end(2)
    for h in range(3):
        f_copy(h, 1 - c).wait_recv()
    for at, nn in enumerate(blocks):
        fg[pl.ds(mult(nn, BW), BW), :] = fl[at * BW : (at + 1) * BW, :]
    ft[...] = fg[...].T
    f_out[...] = ft[pl.ds(mult(c, BW), BW), :]

    for h in range(3):
        f_copy(h, c).wait_send()
    for m in every:
        ag(*m).wait_send()
    for st in range(4):
        reduce_drain(st)
    for m in slices + z_slices:
        slice_copy(*m).wait_send()
    for nn in peers:
        pb_copy(nn).wait_send()
        pb_relay(nn, c).wait_send()
    for kk in range(8):
        relay(kk).wait_send()


def on_device(vectors, reflectors, triangle, energies):
    vm = pl.BlockSpec(memory_space=pltpu.VMEM)
    hbm = pl.BlockSpec(memory_space=pl.ANY)
    dma = pltpu.SemaphoreType.DMA
    return pl.pallas_call(
        kernel,
        out_shape=(
            pltpu.VMEM((ROWS, NC), F32),
            pltpu.VMEM((BW, FB), F32),
        ),
        in_specs=[hbm, hbm, hbm, hbm],
        out_specs=(vm, vm),
        scratch_shapes=[
            pltpu.VMEM((KP, NC), F32),
            pltpu.VMEM((KP, NB), F32),
            pltpu.VMEM((KP, 128), F32),
            pltpu.VMEM((NB, NB), F32),
            pltpu.VMEM((1, ROWS), F32),
            pltpu.VMEM((2, NB, KP), BF16),
            pltpu.VMEM((2, KP, NB), BF16),
            pltpu.VMEM((2, NB, KP), BF16),
            pltpu.VMEM((NB, NC), F32),
            pltpu.VMEM((2, NB, NB), BF16),
            pltpu.VMEM((2, NB, NC), BF16),
            pltpu.VMEM((2, KP, NC), BF16),
            pltpu.VMEM((FB, KP), F32),
            pltpu.VMEM((FB, NB), F32),
            pltpu.VMEM((1, KP), F32),
            *[pltpu.VMEM((m, NC), F32) for m in (NB,) + PARTS],
            *[pltpu.VMEM((m // 2, NC), F32) for m in (NB,) + PARTS],
            *[pltpu.VMEM((8, m // 2, 128), F32) for m in (NB,) + PARTS],
            pltpu.VMEM((NB, NC), F32),
            pltpu.VMEM((2 * PARTS[0], KP), BF16),
            pltpu.VMEM((FB, 128), F32),
            pltpu.VMEM((FB, 128), F32),
            pltpu.VMEM((128, FB), F32),
            dma((8,)), dma((28,)), dma((64,)), dma((16,)), dma((16,)),
            dma((32,)), dma((32,)), dma((7,)), dma((8,)), dma((8,)), dma((8,)),
            dma((16,)), dma((16,)), dma((3,)), dma((3,)),
        ],
        compiler_params=pltpu.CompilerParams(
            collective_id=0, has_side_effects=True, vmem_limit_bytes=50 * 2**20
        ),
        name="reflect_fock",
    )(vectors, reflectors, triangle, energies[None, :])


def solution(mesh):
    return jax.shard_map(
        on_device,
        mesh=mesh,
        in_specs=(P("wide", "narrow"), P("wide", None), P(), P("wide")),
        out_specs=(P("wide", "narrow"), P(("narrow", "wide"), None)),
        check_vma=False,
    )
```

```python
import functools

import jax
import jax.numpy as jnp
from jax import lax
from jax.experimental import pallas as pl
from jax.experimental.pallas import tpu as pltpu
from jax.sharding import PartitionSpec as P

MESH = pl.DeviceIdType.MESH
F32, BF16 = jnp.float32, jnp.bfloat16
ROWS, KP, NC, NB = 2000, 2048, 1024, 256
FB, OFF, BW = 512, 256, 64
PARTS = (256, 192, 64)
KB = OFF // 128


def dot(a, b):
    return jnp.dot(a, b, preferred_element_type=F32)


def split(x):
    hi = x.astype(BF16)
    return hi, (x - hi.astype(F32)).astype(BF16)


def dot3(a, b):
    return dot(a[0], b[0]) + dot(a[0], b[1]) + dot(a[1], b[0])


def mult(i, m):
    return pl.multiple_of(i * m, m)


def kernel(
    v_hbm, r_hbm, t_hbm, e_hbm, u_out, f_out,
    v, r, vb, t_ref, e_ref, rtr, rt, yt, a3, a4, bb, uu, vbt, pbt, ep, part0, part1, part2, part3, xrecv0, xrecv1, xrecv2,
    rsr0, rsr1, rsr2, rsr3, pfull, ub, fl, fx,
    ld_sem, ag_s, ag_r, xs, xr, rs_s, rs_r, pa_s, pa_r, pr_s, pr_r, pb_s, pb_r, f_s, f_r,
):
    w, n = lax.axis_index("wide"), lax.axis_index("narrow")
    c, k = lax.rem(w, 2), w // 2
    y, zh = lax.rem(n, 4), n // 4
    partner = (w + 1 - 2 * c, n)
    yp, ym = zh * 4 + lax.rem(y + 1, 4), zh * 4 + lax.rem(y + 3, 4)
    base = zh * 4
    zbase = (1 - zh) * 4

    def same_core(kk):
        return (2 * kk + c, n)

    def narrow_peer(nn):
        return (w, nn)

    def remote(src, dst, s, rsem, to):
        return pltpu.make_async_remote_copy(
            src_ref=src, dst_ref=dst, send_sem=s, recv_sem=rsem, device_id=to, device_id_type=MESH
        )

    kk0 = k // 2

    def order(s):
        t1, t0 = (3 - s) // 2, lax.rem(3 - s, 2)
        a, b = kk0 // 2, lax.rem(kk0, 2)
        return 2 * (a + t1 - 2 * a * t1) + b + t0 - 2 * b * t0

    vb_load = pltpu.make_async_copy(v_hbm.at[:, pl.ds(OFF, 128)], vb.at[pl.ds(0, ROWS)], ld_sem.at[0])
    r_load = pltpu.make_async_copy(r_hbm, r.at[pl.ds(0, ROWS)], ld_sem.at[1])

    def v_load(i):
        cols = pl.ds(mult(i, 256), 256)
        return pltpu.make_async_copy(v_hbm.at[:, cols], v.at[pl.ds(0, ROWS), cols], ld_sem.at[2 + i])

    t_load = pltpu.make_async_copy(t_hbm, t_ref, ld_sem.at[6])
    e_load = pltpu.make_async_copy(e_hbm, e_ref, ld_sem.at[7])
    vb_load.start()
    r_load.start()
    for s in range(4):
        v_load(order(s)).start()
    t_load.start()
    e_load.start()

    barrier = pltpu.get_barrier_semaphore()
    pl.semaphore_signal(barrier, inc=1, device_id=partner, device_id_type=MESH)
    for d in range(1, 8):
        pl.semaphore_signal(barrier, inc=1, device_id=same_core(lax.rem(k + d, 8)), device_id_type=MESH)
        pl.semaphore_signal(barrier, inc=1, device_id=narrow_peer(lax.rem(n + d, 8)), device_id_type=MESH)

    vb[ROWS:, :] = jnp.zeros((KP - ROWS, 128), F32)
    r[ROWS:, :] = jnp.zeros((KP - ROWS, NB), F32)
    v[ROWS:, :] = jnp.zeros((KP - ROWS, NC), F32)

    vb_load.wait()
    own = pl.ds(mult(n, BW), BW)
    for i in range(KP // 128):
        vbt[own, i * 128 : (i + 1) * 128] = vb[i * 128 : (i + 1) * 128, :].T[:BW, :]
    pl.semaphore_wait(barrier, 15)

    def ag(src_n, o, cnt, to, slot):
        rows = pl.ds(mult(src_n * 8 + o, 8), 8 * cnt)
        return remote(vbt.at[rows], vbt.at[rows], ag_s.at[slot], ag_r.at[src_n * 8 + o], narrow_peer(to))

    def arrived(src_n, o, cnt):
        ag(src_n, o, cnt, yp, 0).wait_recv()

    zp = zbase + y
    zyp, zym = zbase + lax.rem(y + 1, 4), zbase + lax.rem(y + 3, 4)
    y2, zy2 = base + lax.rem(y + 2, 4), zbase + lax.rem(y + 2, 4)
    z_sends = [(n, 2 * q, 2, zp, q) for q in range(4)]
    zx_sends = [(ym, 7, 1, zp, 4), (yp, 7, 1, zp, 5), (y2, 7, 1, zp, 6)]
    y_sends = [(n, 0, 4, yp, 7), (n, 0, 4, ym, 8), (n, 4, 4, yp, 9), (n, 4, 4, ym, 10)]
    y_fwds = [(ym, 0, 2, yp, 11), (yp, 2, 2, ym, 12), (ym, 4, 2, yp, 13), (yp, 6, 2, ym, 14)]
    p_sends = [
        (zp, 0, 2, yp, 15), (zp, 0, 2, ym, 16), (zp, 2, 2, yp, 17), (zp, 2, 2, ym, 18), (zp, 4, 2, yp, 19),
        (zp, 4, 2, ym, 20), (zp, 6, 1, yp, 25), (zp, 6, 1, ym, 26),
    ]
    p_fwds = [(zym, 0, 2, yp, 21), (zyp, 2, 2, ym, 22), (zym, 4, 1, yp, 23), (zyp, 5, 1, ym, 24), (zym, 6, 1, yp, 27)]
    every = z_sends + zx_sends + y_sends + y_fwds + p_sends + p_fwds

    def go(messages):
        for m in messages:
            ag(*m).start()

    go(z_sends[:1] + y_sends)

    r_load.wait()

    @pl.loop(0, 4)
    def _(i):
        rows = pl.ds(mult(i, 512), 512)
        hi, lo = split(r[rows, :])
        rtr[0, :, rows] = hi.T
        rtr[1, :, rows] = lo.T

    part, xrecv = (part0, part1, part2, part3), (xrecv0, xrecv1, xrecv2)
    rsr = (rsr0, rsr1, rsr2, rsr3)
    half_rows = (128, PARTS[0] // 2, PARTS[1] // 2, PARTS[2])
    myrows = pl.ds(mult(c, 128), 128)
    hisrows = pl.ds(mult(1 - c, 128), 128)

    def mine(st):
        return pl.ds(mult(c if st < 3 else 0, half_rows[st]), half_rows[st])

    def his(st):
        return pl.ds(mult(1 - c, half_rows[st]), half_rows[st])

    def x_copy(st, i):
        cols = pl.ds(mult(i, 256), 256)
        return remote(
            part[st].at[his(st), cols], xrecv[st].at[:, cols], xs.at[st * 4 + i], xr.at[st * 4 + i], partner
        )

    def rs_copy(st, kk):
        return remote(
            part[st].at[mine(st), pl.ds(mult(kk, 128), 128)], rsr[st].at[k], rs_s.at[st * 8 + kk],
            rs_r.at[st * 8 + k], same_core(kk),
        )

    def scatter(st, i):
        for t in range(2):
            kk = 2 * i + t

            @pl.when(kk != k)
            def _():
                rs_copy(st, kk).start()

    def finish(st, i):
        cols = pl.ds(mult(i, 256), 256)
        x_copy(st, i).wait_recv()
        part[st][mine(st), cols] = part[st][mine(st), cols] + xrecv[st][:, cols]
        scatter(st, i)

    def reduce_start(st, compute, hooks=()):
        @pl.loop(0, 4)
        def _(s):
            i = order(s)
            part[st][:, pl.ds(mult(i, 256), 256)] = compute(i)
            x_copy(st, i).start()

            @pl.when(s >= 1)
            def _():
                finish(st, order(s - 1))

            for at, hook in hooks:

                @pl.when(s == at)
                def _():
                    hook()

    def reduce_end(st):
        total = part[st][mine(st), pl.ds(mult(k, 128), 128)]
        for d in range(1, 8):
            kk = lax.rem(k + d, 8)
            remote(rsr[st].at[kk], rsr[st].at[kk], rs_s.at[st * 8], rs_r.at[st * 8 + kk], partner).wait_recv()
            total = total + rsr[st][kk]
        return total

    def reduce_drain(st):
        for i in range(4 if st < 3 else 0):
            x_copy(st, i).wait_send()
        for d in range(1, 8):
            rs_copy(st, lax.rem(k + d, 8)).wait_send()

    def project(i):
        v_load(i).wait()
        cols = pl.ds(mult(i, 256), 256)
        hi, lo = split(v[:, cols])
        uu[0, :, cols] = hi
        uu[1, :, cols] = lo
        return dot3((rtr[0], rtr[1]), (hi, lo))

    reduce_start(0, project)

    t_load.wait()
    e_load.wait()
    ep[...] = jnp.zeros((1, KP), F32)
    ep[:, :ROWS] = e_ref[...]
    tt = split(t_ref[...])
    ttt = split(t_ref[...].T)

    @pl.loop(0, 2)
    def _(i):
        rows = pl.ds(mult(i, 1024), 1024)
        hi, lo = split(dot3(split(r[rows, :]), tt))
        rt[0, rows, :] = hi
        rt[1, rows, :] = lo

        @pl.when(i == 0)
        def _():
            finish(0, order(3))
            go(z_sends[1:2])

    @pl.loop(0, 2)
    def _(i):
        rows = pl.ds(mult(i, 1024), 1024)
        hi, lo = split(dot3(ttt, (rtr[0, :, rows], rtr[1, :, rows])) * ep[:, rows])
        yt[0, :, rows] = hi
        yt[1, :, rows] = lo

    x, zl = lax.rem(k, 4), k // 4
    kz = (1 - zl) * 4 + x

    def slice_copy(src_k, to_k, slot):
        cols = pl.ds(mult(src_k, 128), 128)
        return remote(
            pfull.at[myrows, cols], pfull.at[myrows, cols], pa_s.at[slot], pa_r.at[src_k], same_core(to_k)
        )

    x_peers = [zl * 4 + lax.rem(x + d, 4) for d in (1, 3, 2)]
    slices = [(k, kz, 0)] + [(k, kx, 1 + d) for d, kx in enumerate(x_peers)]
    z_slices = [(kz, kx, 4 + d) for d, kx in enumerate(x_peers)]

    def slice_here(kk):
        slice_copy(kk, kz, 0).wait_recv()

    def relay(kk):
        cols = pl.ds(mult(kk, 128), 128)
        return remote(
            pfull.at[myrows, cols], pfull.at[myrows, cols], pr_s.at[kk], pr_r.at[kk], partner
        )

    def own_slice():
        pfull[myrows, pl.ds(mult(k, 128), 128)] = reduce_end(0)
        for m in slices:
            slice_copy(*m).start()

        relay(k).start()
        go(z_sends[2:])

    @pl.loop(0, 4)
    def _(i):
        cols = pl.ds(mult(i, 256), 256)
        a3[:, cols] = dot3((yt[0], yt[1]), (uu[0, :, cols], uu[1, :, cols]))

        @pl.when(i == 1)
        def _():
            arrived(ym, 0, 4)
            arrived(yp, 0, 4)
            go(y_fwds[:2])
            own_slice()

        @pl.when(i == 2)
        def _():
            arrived(ym, 4, 4)
            arrived(yp, 4, 4)
            go(y_fwds[2:])

    hi, lo = split(dot3((yt[0], yt[1]), (rt[0], rt[1])))
    a4[0] = hi
    a4[1] = lo
    slice_here(kz)
    for m in z_slices:
        slice_copy(*m).start()
    relay(kz).start()
    arrived(zp, 0, 2)
    go(p_sends[:2])
    for kx in x_peers:
        slice_here(kx)
        relay(kx).start()

    def relay_in(kk):
        cols = pl.ds(mult(kk, 128), 128)
        return remote(pfull.at[hisrows, cols], pfull.at[hisrows, cols], pr_s.at[0], pr_r.at[kk], partner)

    def slice_arrived(kk):
        relay_in(kk).wait_recv()

    def pb_rows(nn, cc):
        return pbt.at[pl.ds(mult(2 * nn + cc, 32), 32)]

    def pb_copy(nn):
        return remote(pb_rows(n, c), pb_rows(n, c), pb_s.at[nn], pb_r.at[n], narrow_peer(nn))

    def pb_in(nn):
        return remote(pb_rows(nn, c), pb_rows(nn, c), pb_s.at[0], pb_r.at[nn], partner)

    def pb_relay(nn, cc):
        return remote(pb_rows(nn, cc), pb_rows(nn, cc), pb_s.at[8 + nn], pb_r.at[8 + nn], partner)

    peers = [base + lax.rem(y + d, 4) for d in (1, 3, 2)] + [zp, zyp, zym, zy2]

    def pb_send():
        for j in range(2):
            pbt[own, j * 128 : (j + 1) * 128] = pfull[j * 128 : (j + 1) * 128, OFF : OFF + 128].T[:BW, :]
        for nn in peers:
            pb_copy(nn).start()

    blocks = [base + d for d in range(4)] + [zp, zyp, zym, zy2]
    firsts = (0, PARTS[0], PARTS[0] + PARTS[1])

    def sources(h):
        if h == 0:
            return [pl.ds(mult(zh, 4 * BW), 4 * BW)]
        return [pl.ds(mult(nn, BW), BW) for nn in (blocks[4:7] if h == 1 else blocks[7:])]

    def scaled(h):
        at, m = 0, PARTS[h]
        for src in sources(h):
            hi, lo = split(vbt[src, :] * ep[...])
            ub[at : at + hi.shape[0], :] = hi
            ub[m + at : m + at + hi.shape[0], :] = lo
            at += hi.shape[0]

    for kx in [k] + x_peers:
        slice_arrived(kx)

    @pl.when((zl == 1) & (kz != KB))
    def _():
        slice_here(KB)
        relay(KB).start()

    def block_columns():
        @pl.when(zl == 1)
        def _():
            slice_arrived(KB)

        pb_send()
        arrived(zp, 2, 2)
        go(p_sends[2:4] + zx_sends[:2])
        arrived(zp, 4, 2)
        go(p_sends[4:6])

    z_peers = [(1 - zl) * 4 + lax.rem(x + d, 4) for d in (1, 3, 2)]

    def pb_pass(some):
        for nn in some:
            pb_in(nn).wait_recv()
            pb_relay(nn, c).start()

    def others():
        for kx in z_peers:

            @pl.when((zl == 0) | (kx != KB))
            def _():
                slice_here(kx)
                relay(kx).start()

        for o in (0, 2, 4, 6):
            arrived(y2, o, 2)
        go(zx_sends[2:])
        scaled(0)
        arrived(zp, 6, 2)
        go(p_sends[6:])
        arrived(zym, 0, 2)
        go(p_fwds[:1])
        for kx in [kz] + z_peers:

            @pl.when((zl == 0) | (kx != KB))
            def _():
                slice_arrived(kx)

    @pl.loop(0, 4)
    def _(s):
        cols = pl.ds(mult(lax.rem(2 * zl + s, 4), 256), 256)
        p = split(pfull[:, cols])
        u = v[:ROWS, cols] - dot3((rt[0, :ROWS, :], rt[1, :ROWS, :]), p)
        u_out[:, cols] = u
        hi, lo = split(u)
        uu[0, :ROWS, cols] = hi
        uu[1, :ROWS, cols] = lo
        hi, lo = split(a3[:, cols] - dot3((a4[0], a4[1]), p))
        bb[0, :, cols] = hi
        bb[1, :, cols] = lo

        @pl.when(s == 0)
        def _():
            block_columns()

        @pl.when(s == 1)
        def _():
            others()

        @pl.when(s == 2)
        def _():
            pb_pass(peers[:3])

    def f_rows(h, cc):
        first = firsts[h] + cc * half_rows[1 + h] if h < 2 else firsts[2]
        return fl.at[pl.ds(pl.multiple_of(first, 32), half_rows[1 + h])]

    def f_copy(h, cc):
        return remote(f_rows(h, cc), f_rows(h, cc) if h < 2 else fx, f_s.at[h], f_r.at[h], partner)

    def pb_part(h, i):
        cols = pl.ds(mult(i, 256), 256)
        return dot3(split(jnp.concatenate([pbt[src, :] for src in sources(h)], axis=0)), (bb[0, :, cols], bb[1, :, cols]))

    def main_part(h, i):
        m = PARTS[h]
        cols = pl.ds(mult(i, 256), 256)
        if h < 2:
            return dot3((ub[:m], ub[m : 2 * m]), (uu[0, :, cols], uu[1, :, cols]))
        both = dot(ub[: 2 * m], uu[0, :, cols])
        return both[:m] + both[m:] + dot(ub[:m], uu[1, :, cols])

    def pass_some():
        arrived(zyp, 2, 2)
        go(p_fwds[1:2])
        pb_pass(peers[3:])

    def pass_last():
        arrived(zym, 4, 2)
        arrived(zyp, 4, 2)
        go(p_fwds[2:4])

    def fock_end(h):
        f_rows(h, c)[...] = reduce_end(1 + h)
        f_copy(h, c).start()

    for nn in peers[:3]:
        pb_relay(nn, 1 - c).wait_recv()
    reduce_start(1, lambda i: main_part(0, i) - pb_part(0, i), [(1, pass_some), (3, pass_last)])
    arrived(zym, 6, 1)
    go(p_fwds[4:])
    for nn in peers[3:]:
        pb_relay(nn, 1 - c).wait_recv()
    for src, o, cnt in ((zym, 2, 2), (zym, 7, 1), (zyp, 0, 2), (zyp, 6, 1), (zyp, 7, 1)):
        arrived(src, o, cnt)
    scaled(1)
    reduce_start(2, lambda i: main_part(1, i) - pb_part(1, i), [(0, lambda: finish(1, order(3)))])
    for o, cnt in ((0, 2), (2, 2), (4, 1), (5, 1), (6, 1), (7, 1)):
        arrived(zy2, o, cnt)
    scaled(2)
    @pl.loop(0, 4)
    def _(s):
        i = order(s)
        part3[:, pl.ds(mult(i, 256), 256)] = main_part(2, i) - pb_part(2, i)

        @pl.when(s == 0)
        def _():
            finish(2, order(3))

        scatter(3, i)

    fock_end(0)
    fock_end(1)
    fock_end(2)
    for h in range(3):
        f_copy(h, 1 - c).wait_recv()
    f_out[: firsts[2], :] = fl[: firsts[2], :]
    f_out[firsts[2] :, :] = fl[firsts[2] :, :] + fx[...]

    for h in range(3):
        f_copy(h, c).wait_send()
    for m in every:
        ag(*m).wait_send()
    for st in range(4):
        reduce_drain(st)
    for m in slices + z_slices:
        slice_copy(*m).wait_send()
    for nn in peers:
        pb_copy(nn).wait_send()
        pb_relay(nn, c).wait_send()
    for kk in range(8):
        relay(kk).wait_send()


def store(u, f, u_hbm, f_hbm, fg, ft, fo, sem):
    copies = []
    for i in range(10):
        rows = pl.ds(200 * i, 200)
        copies.append(pltpu.make_async_copy(u.at[rows], u_hbm.at[rows], sem.at[i]))
    for copy in copies:
        copy.start()
    c, n = lax.rem(lax.axis_index("wide"), 2), lax.axis_index("narrow")
    y, base, zbase = lax.rem(n, 4), n // 4 * 4, (1 - n // 4) * 4
    zp, zyp, zym, zy2 = [zbase + lax.rem(y + d, 4) for d in (0, 1, 3, 2)]
    for at, nn in enumerate([base + d for d in range(4)] + [zp, zyp, zym, zy2]):
        fg[pl.ds(mult(nn, BW), BW), :] = f[at * BW : (at + 1) * BW, :]
    ft[...] = fg[...].T
    fo[...] = ft[pl.ds(mult(c, BW), BW), :]
    copies.append(pltpu.make_async_copy(fo, f_hbm, sem.at[10]))
    copies[-1].start()
    for copy in copies:
        copy.wait()


def on_device(vectors, reflectors, triangle, energies):
    vm = pl.BlockSpec(memory_space=pltpu.VMEM)
    hbm = pl.BlockSpec(memory_space=pl.ANY)
    dma = pltpu.SemaphoreType.DMA
    u, f = pl.pallas_call(
        kernel,
        out_shape=(
            pltpu.VMEM((ROWS, NC), F32),
            pltpu.VMEM((FB, 128), F32),
        ),
        in_specs=[hbm, hbm, hbm, hbm],
        out_specs=(vm, vm),
        scratch_shapes=[
            pltpu.VMEM((KP, NC), F32),
            pltpu.VMEM((KP, NB), F32),
            pltpu.VMEM((KP, 128), F32),
            pltpu.VMEM((NB, NB), F32),
            pltpu.VMEM((1, ROWS), F32),
            pltpu.VMEM((2, NB, KP), BF16),
            pltpu.VMEM((2, KP, NB), BF16),
            pltpu.VMEM((2, NB, KP), BF16),
            pltpu.VMEM((NB, NC), F32),
            pltpu.VMEM((2, NB, NB), BF16),
            pltpu.VMEM((2, NB, NC), BF16),
            pltpu.VMEM((2, KP, NC), BF16),
            pltpu.VMEM((FB, KP), F32),
            pltpu.VMEM((FB, NB), F32),
            pltpu.VMEM((1, KP), F32),
            *[pltpu.VMEM((m, NC), F32) for m in (NB,) + PARTS],
            *[pltpu.VMEM((m // 2, NC), F32) for m in (NB,) + PARTS[:2]],
            *[pltpu.VMEM((8, m // 2, 128), F32) for m in (NB,) + PARTS[:2]],
            pltpu.VMEM((8, PARTS[2], 128), F32),
            pltpu.VMEM((NB, NC), F32),
            pltpu.VMEM((2 * PARTS[0], KP), BF16),
            pltpu.VMEM((FB, 128), F32),
            pltpu.VMEM((PARTS[2], 128), F32),
            dma((8,)), dma((28,)), dma((64,)), dma((16,)), dma((16,)),
            dma((32,)), dma((32,)), dma((7,)), dma((8,)), dma((8,)), dma((8,)),
            dma((16,)), dma((16,)), dma((3,)), dma((3,)),
        ],
        compiler_params=pltpu.CompilerParams(
            collective_id=0, has_side_effects=True, vmem_limit_bytes=50 * 2**20
        ),
        name="reflect_fock",
    )(vectors, reflectors, triangle, energies[None, :])
    return pl.pallas_call(
        store,
        out_shape=(
            jax.ShapeDtypeStruct((ROWS, NC), F32),
            jax.ShapeDtypeStruct((BW, FB), F32),
        ),
        in_specs=[vm, vm],
        out_specs=(hbm, hbm),
        scratch_shapes=[
            pltpu.VMEM((FB, 128), F32),
            pltpu.VMEM((128, FB), F32),
            pltpu.VMEM((BW, FB), F32),
            dma((11,)),
        ],
        compiler_params=pltpu.CompilerParams(vmem_limit_bytes=2**21),
        name="store",
    )(u, f)


def solution(mesh):
    return jax.shard_map(
        on_device,
        mesh=mesh,
        in_specs=(P("wide", "narrow"), P("wide", None), P(), P("wide")),
        out_specs=(P("wide", "narrow"), P(("narrow", "wide"), None)),
        check_vma=False,
    )
```

```python
import functools

import jax
import jax.numpy as jnp
from jax import lax
from jax.experimental import pallas as pl
from jax.experimental.pallas import tpu as pltpu
from jax.sharding import PartitionSpec as P

MESH = pl.DeviceIdType.MESH
F32, BF16 = jnp.float32, jnp.bfloat16
ROWS, KP, NC, NB = 2000, 2048, 1024, 256
FB, OFF, BW = 512, 256, 64
PARTS = (256, 192, 64)
KB = OFF // 128


def dot(a, b):
    return jnp.dot(a, b, preferred_element_type=F32)


def split(x):
    hi = x.astype(BF16)
    return hi, (x - hi.astype(F32)).astype(BF16)


def dot3(a, b):
    return dot(a[0], b[0]) + dot(a[0], b[1]) + dot(a[1], b[0])


def mult(i, m):
    return pl.multiple_of(i * m, m)


def kernel(
    v_hbm, r_hbm, t_hbm, e_hbm, u_out, f_out,
    v, r, vb, t_ref, e_ref, rtr, rt, yt, a3, a4, bb, uu, vbt, pbt, ep, part0, part1, part2, part3, xrecv0, xrecv1, xrecv2,
    rsr0, rsr1, rsr2, rsr3, pfull, ub, fl, fx,
    ld_sem, ag_s, ag_r, xs, xr, rs_s, rs_r, pa_s, pa_r, pr_s, pr_r, pb_s, pb_r, f_s, f_r,
):
    w, n = lax.axis_index("wide"), lax.axis_index("narrow")
    c, k = lax.rem(w, 2), w // 2
    y, zh = lax.rem(n, 4), n // 4
    partner = (w + 1 - 2 * c, n)
    yp, ym = zh * 4 + lax.rem(y + 1, 4), zh * 4 + lax.rem(y + 3, 4)
    base = zh * 4
    zbase = (1 - zh) * 4

    def same_core(kk):
        return (2 * kk + c, n)

    def narrow_peer(nn):
        return (w, nn)

    def remote(src, dst, s, rsem, to):
        return pltpu.make_async_remote_copy(
            src_ref=src, dst_ref=dst, send_sem=s, recv_sem=rsem, device_id=to, device_id_type=MESH
        )

    kk0 = k // 2

    def order(s):
        t1, t0 = (3 - s) // 2, lax.rem(3 - s, 2)
        a, b = kk0 // 2, lax.rem(kk0, 2)
        return 2 * (a + t1 - 2 * a * t1) + b + t0 - 2 * b * t0

    vb_load = pltpu.make_async_copy(v_hbm.at[:, pl.ds(OFF, 128)], vb.at[pl.ds(0, ROWS)], ld_sem.at[0])
    r_load = pltpu.make_async_copy(r_hbm, r.at[pl.ds(0, ROWS)], ld_sem.at[1])

    def v_load(i):
        cols = pl.ds(mult(i, 256), 256)
        return pltpu.make_async_copy(v_hbm.at[:, cols], v.at[pl.ds(0, ROWS), cols], ld_sem.at[2 + i])

    t_load = pltpu.make_async_copy(t_hbm, t_ref, ld_sem.at[6])
    e_load = pltpu.make_async_copy(e_hbm, e_ref, ld_sem.at[7])
    vb_load.start()
    r_load.start()
    for s in range(4):
        v_load(order(s)).start()
    t_load.start()
    e_load.start()

    barrier = pltpu.get_barrier_semaphore()
    pl.semaphore_signal(barrier, inc=1, device_id=partner, device_id_type=MESH)
    for d in range(1, 8):
        pl.semaphore_signal(barrier, inc=1, device_id=same_core(lax.rem(k + d, 8)), device_id_type=MESH)
        pl.semaphore_signal(barrier, inc=1, device_id=narrow_peer(lax.rem(n + d, 8)), device_id_type=MESH)

    vb[ROWS:, :] = jnp.zeros((KP - ROWS, 128), F32)
    r[ROWS:, :] = jnp.zeros((KP - ROWS, NB), F32)
    v[ROWS:, :] = jnp.zeros((KP - ROWS, NC), F32)

    vb_load.wait()
    own = pl.ds(mult(n, BW), BW)
    for i in range(KP // 128):
        vbt[own, i * 128 : (i + 1) * 128] = vb[i * 128 : (i + 1) * 128, :].T[:BW, :]
    pl.semaphore_wait(barrier, 15)

    def ag(src_n, o, cnt, to, slot):
        rows = pl.ds(mult(src_n * 8 + o, 8), 8 * cnt)
        return remote(vbt.at[rows], vbt.at[rows], ag_s.at[slot], ag_r.at[src_n * 8 + o], narrow_peer(to))

    def arrived(src_n, o, cnt):
        ag(src_n, o, cnt, yp, 0).wait_recv()

    zp = zbase + y
    zyp, zym = zbase + lax.rem(y + 1, 4), zbase + lax.rem(y + 3, 4)
    y2, zy2 = base + lax.rem(y + 2, 4), zbase + lax.rem(y + 2, 4)
    z_sends = [(n, 2 * q, 2, zp, q) for q in range(4)]
    zx_sends = [(ym, 7, 1, zp, 4), (yp, 7, 1, zp, 5), (y2, 7, 1, zp, 6)]
    y_sends = [(n, 0, 4, yp, 7), (n, 0, 4, ym, 8), (n, 4, 4, yp, 9), (n, 4, 4, ym, 10)]
    y_fwds = [(ym, 0, 2, yp, 11), (yp, 2, 2, ym, 12), (ym, 4, 2, yp, 13), (yp, 6, 2, ym, 14)]
    p_sends = [
        (zp, 0, 2, yp, 15), (zp, 0, 2, ym, 16), (zp, 2, 2, yp, 17), (zp, 2, 2, ym, 18), (zp, 4, 2, yp, 19),
        (zp, 4, 2, ym, 20), (zp, 6, 1, yp, 25), (zp, 6, 1, ym, 26),
    ]
    p_fwds = [(zym, 0, 2, yp, 21), (zyp, 2, 2, ym, 22), (zym, 4, 1, yp, 23), (zyp, 5, 1, ym, 24), (zym, 6, 1, yp, 27)]
    every = z_sends + zx_sends + y_sends + y_fwds + p_sends + p_fwds

    def go(messages):
        for m in messages:
            ag(*m).start()

    go(z_sends[:1] + y_sends)

    r_load.wait()

    @pl.loop(0, 4)
    def _(i):
        rows = pl.ds(mult(i, 512), 512)
        hi, lo = split(r[rows, :])
        rtr[0, :, rows] = hi.T
        rtr[1, :, rows] = lo.T

    part, xrecv = (part0, part1, part2, part3), (xrecv0, xrecv1, xrecv2)
    rsr = (rsr0, rsr1, rsr2, rsr3)
    half_rows = (128, PARTS[0] // 2, PARTS[1] // 2, PARTS[2])
    myrows = pl.ds(mult(c, 128), 128)
    hisrows = pl.ds(mult(1 - c, 128), 128)

    def mine(st):
        return pl.ds(mult(c if st < 3 else 0, half_rows[st]), half_rows[st])

    def his(st):
        return pl.ds(mult(1 - c, half_rows[st]), half_rows[st])

    def x_copy(st, i):
        cols = pl.ds(mult(i, 256), 256)
        return remote(
            part[st].at[his(st), cols], xrecv[st].at[:, cols], xs.at[st * 4 + i], xr.at[st * 4 + i], partner
        )

    def rs_copy(st, kk):
        return remote(
            part[st].at[mine(st), pl.ds(mult(kk, 128), 128)], rsr[st].at[k], rs_s.at[st * 8 + kk],
            rs_r.at[st * 8 + k], same_core(kk),
        )

    def scatter(st, i):
        for t in range(2):
            kk = 2 * i + t

            @pl.when(kk != k)
            def _():
                rs_copy(st, kk).start()

    def finish(st, i):
        cols = pl.ds(mult(i, 256), 256)
        x_copy(st, i).wait_recv()
        part[st][mine(st), cols] = part[st][mine(st), cols] + xrecv[st][:, cols]
        scatter(st, i)

    def reduce_start(st, compute, hooks=()):
        @pl.loop(0, 4)
        def _(s):
            i = order(s)
            part[st][:, pl.ds(mult(i, 256), 256)] = compute(i)
            x_copy(st, i).start()

            @pl.when(s >= 1)
            def _():
                finish(st, order(s - 1))

            for at, hook in hooks:

                @pl.when(s == at)
                def _():
                    hook()

    def reduce_end(st):
        total = part[st][mine(st), pl.ds(mult(k, 128), 128)]
        for d in range(1, 8):
            kk = lax.rem(k + d, 8)
            remote(rsr[st].at[kk], rsr[st].at[kk], rs_s.at[st * 8], rs_r.at[st * 8 + kk], partner).wait_recv()
            total = total + rsr[st][kk]
        return total

    def reduce_drain(st):
        for i in range(4 if st < 3 else 0):
            x_copy(st, i).wait_send()
        for d in range(1, 8):
            rs_copy(st, lax.rem(k + d, 8)).wait_send()

    def project(i):
        v_load(i).wait()
        cols = pl.ds(mult(i, 256), 256)
        hi, lo = split(v[:, cols])
        uu[0, :, cols] = hi
        uu[1, :, cols] = lo
        return dot3((rtr[0], rtr[1]), (hi, lo))

    reduce_start(0, project)

    t_load.wait()
    e_load.wait()
    ep[...] = jnp.zeros((1, KP), F32)
    ep[:, :ROWS] = e_ref[...]
    tt = split(t_ref[...])
    ttt = split(t_ref[...].T)

    @pl.loop(0, 2)
    def _(i):
        rows = pl.ds(mult(i, 1024), 1024)
        hi, lo = split(dot3(split(r[rows, :]), tt))
        rt[0, rows, :] = hi
        rt[1, rows, :] = lo

        @pl.when(i == 0)
        def _():
            finish(0, order(3))
            go(z_sends[1:2])

    @pl.loop(0, 2)
    def _(i):
        rows = pl.ds(mult(i, 1024), 1024)
        hi, lo = split(dot3(ttt, (rtr[0, :, rows], rtr[1, :, rows])) * ep[:, rows])
        yt[0, :, rows] = hi
        yt[1, :, rows] = lo

    x, zl = lax.rem(k, 4), k // 4
    kz = (1 - zl) * 4 + x

    def slice_copy(src_k, to_k, slot):
        cols = pl.ds(mult(src_k, 128), 128)
        return remote(
            pfull.at[myrows, cols], pfull.at[myrows, cols], pa_s.at[slot], pa_r.at[src_k], same_core(to_k)
        )

    x_peers = [zl * 4 + lax.rem(x + d, 4) for d in (1, 3, 2)]
    slices = [(k, kz, 0)] + [(k, kx, 1 + d) for d, kx in enumerate(x_peers)]
    z_slices = [(kz, kx, 4 + d) for d, kx in enumerate(x_peers)]

    def slice_here(kk):
        slice_copy(kk, kz, 0).wait_recv()

    def relay(kk):
        cols = pl.ds(mult(kk, 128), 128)
        return remote(
            pfull.at[myrows, cols], pfull.at[myrows, cols], pr_s.at[kk], pr_r.at[kk], partner
        )

    def own_slice():
        pfull[myrows, pl.ds(mult(k, 128), 128)] = reduce_end(0)
        for m in slices:
            slice_copy(*m).start()

        relay(k).start()
        go(z_sends[2:])

    @pl.loop(0, 4)
    def _(i):
        cols = pl.ds(mult(i, 256), 256)
        a3[:, cols] = dot3((yt[0], yt[1]), (uu[0, :, cols], uu[1, :, cols]))

        @pl.when(i == 1)
        def _():
            arrived(ym, 0, 4)
            arrived(yp, 0, 4)
            go(y_fwds[:2])
            own_slice()

        @pl.when(i == 2)
        def _():
            arrived(ym, 4, 4)
            arrived(yp, 4, 4)
            go(y_fwds[2:])

    hi, lo = split(dot3((yt[0], yt[1]), (rt[0], rt[1])))
    a4[0] = hi
    a4[1] = lo
    slice_here(kz)
    for m in z_slices:
        slice_copy(*m).start()
    relay(kz).start()
    arrived(zp, 0, 2)
    go(p_sends[:2])
    for kx in x_peers:
        slice_here(kx)
        relay(kx).start()

    def relay_in(kk):
        cols = pl.ds(mult(kk, 128), 128)
        return remote(pfull.at[hisrows, cols], pfull.at[hisrows, cols], pr_s.at[0], pr_r.at[kk], partner)

    def slice_arrived(kk):
        relay_in(kk).wait_recv()

    def pb_rows(nn, cc):
        return pbt.at[pl.ds(mult(2 * nn + cc, 32), 32)]

    def pb_copy(nn):
        return remote(pb_rows(n, c), pb_rows(n, c), pb_s.at[nn], pb_r.at[n], narrow_peer(nn))

    def pb_in(nn):
        return remote(pb_rows(nn, c), pb_rows(nn, c), pb_s.at[0], pb_r.at[nn], partner)

    def pb_relay(nn, cc):
        return remote(pb_rows(nn, cc), pb_rows(nn, cc), pb_s.at[8 + nn], pb_r.at[8 + nn], partner)

    peers = [base + lax.rem(y + d, 4) for d in (1, 3, 2)] + [zp, zyp, zym, zy2]

    def pb_send():
        for j in range(2):
            pbt[own, j * 128 : (j + 1) * 128] = pfull[j * 128 : (j + 1) * 128, OFF : OFF + 128].T[:BW, :]
        for nn in peers:
            pb_copy(nn).start()

    blocks = [base + d for d in range(4)] + [zp, zyp, zym, zy2]
    firsts = (0, PARTS[0], PARTS[0] + PARTS[1])

    def sources(h):
        if h == 0:
            return [pl.ds(mult(zh, 4 * BW), 4 * BW)]
        return [pl.ds(mult(nn, BW), BW) for nn in (blocks[4:7] if h == 1 else blocks[7:])]

    def scaled(h):
        at, m = 0, PARTS[h]
        for src in sources(h):
            hi, lo = split(vbt[src, :] * ep[...])
            ub[at : at + hi.shape[0], :] = hi
            ub[m + at : m + at + hi.shape[0], :] = lo
            at += hi.shape[0]

    for kx in [k] + x_peers:
        slice_arrived(kx)

    @pl.when((zl == 1) & (kz != KB))
    def _():
        slice_here(KB)
        relay(KB).start()

    def block_columns():
        @pl.when(zl == 1)
        def _():
            slice_arrived(KB)

        pb_send()
        arrived(zp, 2, 2)
        go(p_sends[2:4] + zx_sends[:2])
        arrived(zp, 4, 2)
        go(p_sends[4:6])

    z_peers = [(1 - zl) * 4 + lax.rem(x + d, 4) for d in (1, 3, 2)]

    def pb_pass(some):
        for nn in some:
            pb_in(nn).wait_recv()
            pb_relay(nn, c).start()

    def others():
        for kx in z_peers:

            @pl.when((zl == 0) | (kx != KB))
            def _():
                slice_here(kx)
                relay(kx).start()

        for o in (0, 2, 4, 6):
            arrived(y2, o, 2)
        go(zx_sends[2:])
        scaled(0)
        arrived(zp, 6, 2)
        go(p_sends[6:])
        arrived(zym, 0, 2)
        go(p_fwds[:1])
        for kx in [kz] + z_peers:

            @pl.when((zl == 0) | (kx != KB))
            def _():
                slice_arrived(kx)

    @pl.loop(0, 4)
    def _(s):
        cols = pl.ds(mult(lax.rem(2 * zl + s, 4), 256), 256)
        p = split(pfull[:, cols])
        u = v[:ROWS, cols] - dot3((rt[0, :ROWS, :], rt[1, :ROWS, :]), p)
        u_out[:, cols] = u
        hi, lo = split(u)
        uu[0, :ROWS, cols] = hi
        uu[1, :ROWS, cols] = lo
        hi, lo = split(a3[:, cols] - dot3((a4[0], a4[1]), p))
        bb[0, :, cols] = hi
        bb[1, :, cols] = lo

        @pl.when(s == 0)
        def _():
            block_columns()

        @pl.when(s == 1)
        def _():
            others()

        @pl.when(s == 2)
        def _():
            pb_pass(peers[:3])

    def f_rows(h, cc):
        first = firsts[h] + cc * half_rows[1 + h] if h < 2 else firsts[2]
        return fl.at[pl.ds(pl.multiple_of(first, 32), half_rows[1 + h])]

    def f_copy(h, cc):
        return remote(f_rows(h, cc), f_rows(h, cc) if h < 2 else fx, f_s.at[h], f_r.at[h], partner)

    def pb_part(h, i):
        cols = pl.ds(mult(i, 256), 256)
        return dot3(split(jnp.concatenate([pbt[src, :] for src in sources(h)], axis=0)), (bb[0, :, cols], bb[1, :, cols]))

    def main_part(h, i):
        m = PARTS[h]
        cols = pl.ds(mult(i, 256), 256)
        if h < 2:
            return dot3((ub[:m], ub[m : 2 * m]), (uu[0, :, cols], uu[1, :, cols]))
        both = dot(ub[: 2 * m], uu[0, :, cols])
        return both[:m] + both[m:] + dot(ub[:m], uu[1, :, cols])

    def pass_some():
        arrived(zyp, 2, 2)
        go(p_fwds[1:2])
        pb_pass(peers[3:])

    def pass_last():
        arrived(zym, 4, 2)
        arrived(zyp, 4, 2)
        go(p_fwds[2:4])

    def fock_end(h):
        f_rows(h, c)[...] = reduce_end(1 + h)
        f_copy(h, c).start()

    for nn in peers[:3]:
        pb_relay(nn, 1 - c).wait_recv()
    reduce_start(1, lambda i: main_part(0, i) - pb_part(0, i), [(1, pass_some), (3, pass_last)])
    finish(1, order(3))
    arrived(zym, 6, 1)
    go(p_fwds[4:])
    for nn in peers[3:]:
        pb_relay(nn, 1 - c).wait_recv()
    for src, o, cnt in ((zym, 2, 2), (zym, 7, 1), (zyp, 0, 2), (zyp, 6, 1), (zyp, 7, 1)):
        arrived(src, o, cnt)
    scaled(1)
    reduce_start(2, lambda i: main_part(1, i) - pb_part(1, i))
    finish(2, order(3))
    for o, cnt in ((0, 2), (2, 2), (4, 1), (5, 1), (6, 1), (7, 1)):
        arrived(zy2, o, cnt)
    fock_end(0)
    scaled(2)
    @pl.loop(0, 4)
    def _(s):
        i = order(s)
        part3[:, pl.ds(mult(i, 256), 256)] = main_part(2, i) - pb_part(2, i)

        scatter(3, i)

    fock_end(1)
    fock_end(2)
    for h in range(3):
        f_copy(h, 1 - c).wait_recv()
    f_out[: firsts[2], :] = fl[: firsts[2], :]
    f_out[firsts[2] :, :] = fl[firsts[2] :, :] + fx[...]

    for h in range(3):
        f_copy(h, c).wait_send()
    for m in every:
        ag(*m).wait_send()
    for st in range(4):
        reduce_drain(st)
    for m in slices + z_slices:
        slice_copy(*m).wait_send()
    for nn in peers:
        pb_copy(nn).wait_send()
        pb_relay(nn, c).wait_send()
    for kk in range(8):
        relay(kk).wait_send()


def store(u, f, u_hbm, f_hbm, fg, ft, fo, sem):
    copies = []
    for i in range(10):
        rows = pl.ds(200 * i, 200)
        copies.append(pltpu.make_async_copy(u.at[rows], u_hbm.at[rows], sem.at[i]))
    for copy in copies:
        copy.start()
    c, n = lax.rem(lax.axis_index("wide"), 2), lax.axis_index("narrow")
    y, base, zbase = lax.rem(n, 4), n // 4 * 4, (1 - n // 4) * 4
    zp, zyp, zym, zy2 = [zbase + lax.rem(y + d, 4) for d in (0, 1, 3, 2)]
    for at, nn in enumerate([base + d for d in range(4)] + [zp, zyp, zym, zy2]):
        fg[pl.ds(mult(nn, BW), BW), :] = f[at * BW : (at + 1) * BW, :]
    ft[...] = fg[...].T
    fo[...] = ft[pl.ds(mult(c, BW), BW), :]
    copies.append(pltpu.make_async_copy(fo, f_hbm, sem.at[10]))
    copies[-1].start()
    for copy in copies:
        copy.wait()


def on_device(vectors, reflectors, triangle, energies):
    vm = pl.BlockSpec(memory_space=pltpu.VMEM)
    hbm = pl.BlockSpec(memory_space=pl.ANY)
    dma = pltpu.SemaphoreType.DMA
    u, f = pl.pallas_call(
        kernel,
        out_shape=(
            pltpu.VMEM((ROWS, NC), F32),
            pltpu.VMEM((FB, 128), F32),
        ),
        in_specs=[hbm, hbm, hbm, hbm],
        out_specs=(vm, vm),
        scratch_shapes=[
            pltpu.VMEM((KP, NC), F32),
            pltpu.VMEM((KP, NB), F32),
            pltpu.VMEM((KP, 128), F32),
            pltpu.VMEM((NB, NB), F32),
            pltpu.VMEM((1, ROWS), F32),
            pltpu.VMEM((2, NB, KP), BF16),
            pltpu.VMEM((2, KP, NB), BF16),
            pltpu.VMEM((2, NB, KP), BF16),
            pltpu.VMEM((NB, NC), F32),
            pltpu.VMEM((2, NB, NB), BF16),
            pltpu.VMEM((2, NB, NC), BF16),
            pltpu.VMEM((2, KP, NC), BF16),
            pltpu.VMEM((FB, KP), F32),
            pltpu.VMEM((FB, NB), F32),
            pltpu.VMEM((1, KP), F32),
            *[pltpu.VMEM((m, NC), F32) for m in (NB,) + PARTS],
            *[pltpu.VMEM((m // 2, NC), F32) for m in (NB,) + PARTS[:2]],
            *[pltpu.VMEM((8, m // 2, 128), F32) for m in (NB,) + PARTS[:2]],
            pltpu.VMEM((8, PARTS[2], 128), F32),
            pltpu.VMEM((NB, NC), F32),
            pltpu.VMEM((2 * PARTS[0], KP), BF16),
            pltpu.VMEM((FB, 128), F32),
            pltpu.VMEM((PARTS[2], 128), F32),
            dma((8,)), dma((28,)), dma((64,)), dma((16,)), dma((16,)),
            dma((32,)), dma((32,)), dma((7,)), dma((8,)), dma((8,)), dma((8,)),
            dma((16,)), dma((16,)), dma((3,)), dma((3,)),
        ],
        compiler_params=pltpu.CompilerParams(
            collective_id=0, has_side_effects=True, vmem_limit_bytes=50 * 2**20
        ),
        name="reflect_fock",
    )(vectors, reflectors, triangle, energies[None, :])
    return pl.pallas_call(
        store,
        out_shape=(
            jax.ShapeDtypeStruct((ROWS, NC), F32),
            jax.ShapeDtypeStruct((BW, FB), F32),
        ),
        in_specs=[vm, vm],
        out_specs=(hbm, hbm),
        scratch_shapes=[
            pltpu.VMEM((FB, 128), F32),
            pltpu.VMEM((128, FB), F32),
            pltpu.VMEM((BW, FB), F32),
            dma((11,)),
        ],
        compiler_params=pltpu.CompilerParams(vmem_limit_bytes=2**21),
        name="store",
    )(u, f)


def solution(mesh):
    return jax.shard_map(
        on_device,
        mesh=mesh,
        in_specs=(P("wide", "narrow"), P("wide", None), P(), P("wide")),
        out_specs=(P("wide", "narrow"), P(("narrow", "wide"), None)),
        check_vma=False,
    )
```
